128 devices in a mesh: row: 16 (over y_lo, x, core), col: 8 (over y_hi, z).
Axes of the slice: x: 4, y: 4 (y_hi: 2, y_lo: 2; y = y_hi * 2 + y_lo), z: 4, core: 2. Of those that a mesh axis runs over, the one named last changes fastest.
Arguments:
- embeddings: float32 [49152, 64], P(('row', 'col')), may hold values from -6 to 6
- inv_length: float32 [64], replicated, may hold values from 0.1 to 0.4
- noise: float32 [49152], P(('row', 'col')), may hold values from 0.1 to 1
- probes: bfloat16 [49152, 256], P(('row', 'col')), may hold values from -1.5 to 1.5
Outputs:
- applied: float32 [49152, 256], P(('row', 'col'))
The draws below stay inside these ranges and needn't reach their ends.
All inputs are finite; a program needn't handle non-finite values.
Results may differ from the reference program's by a relative error of at most 0.0029.
Values may be sent and summed in bfloat16 or wider, within the bound.
No kernel may reach another device: no remote copies, remote signals or barrier semaphores. Data moves between devices by JAX's collectives and lax.ppermute only.
A program may use at most 192 MiB of HBM per device.

```python
import math
import jax
import jax.numpy as jnp
from jax import lax

EMB = 64
PROBES = 256
NPTS = 49152


def block_levels(own_key, extent, pieces, least, largest):
    def one(axis_at, shards_of):
        steps = jax.random.uniform(jax.random.fold_in(jax.random.fold_in(own_key, 6), axis_at), (shards_of,), jnp.float32, least / len(pieces), largest / len(pieces))
        return jnp.repeat(jnp.exp(steps), extent[axis_at] // shards_of).reshape((-1,) + (1,) * (len(extent) - axis_at - 1))

    factor_of = one(*pieces[0])
    for cut in pieces[1:]:
        factor_of = factor_of * one(*cut)
    return factor_of


def centred(stream_key, extent, deviation, most, split=(), kind=jnp.bfloat16):
    entries = deviation * jax.random.normal(stream_key, extent, jnp.float32)
    if split:
        entries = entries * block_levels(stream_key, extent, split, -0.22, 0.18)
    return jnp.clip(entries, -most, most).astype(kind)


def setup_inputs(seed: int = 0) -> dict:
    keys = jax.random.split(jax.random.key(seed), 5)
    return {
        "embeddings": centred(keys[0], (NPTS, EMB), 1.0, 6.0, ((0, 128),), jnp.float32),
        "inv_length": jnp.clip(jnp.exp(jax.random.uniform(keys[1], (EMB,), jnp.float32, math.log(0.1), math.log(0.4))), 0.1, 0.4),
        "noise": jnp.clip(jnp.exp(math.log(1.0) - 2.3025851 * jax.random.uniform(keys[2], (NPTS,), jnp.float32) ** block_levels(keys[2], (NPTS,), ((0, 128),), -0.2, 0.2)), 0.1, 1.0),
        "probes": centred(keys[3], (NPTS, PROBES), 0.25, 1.5, ((0, 128),)),
    }


def reference(embeddings, inv_length, noise, probes):
    scaled = embeddings * inv_length[None, :]
    sq_norm = jnp.sum(scaled * scaled, axis=1)
    total = scaled.shape[0]
    blocks = total // 256

    def one_block(index):
        start = (index * 256).astype(jnp.int32)
        rows = lax.dynamic_slice_in_dim(scaled, start, 256, 0)
        row_sq = lax.dynamic_slice_in_dim(sq_norm, start, 256, 0)
        gram = jnp.dot(rows, scaled.T, precision=lax.Precision.HIGHEST, preferred_element_type=jnp.float32)
        dist = row_sq[:, None] + sq_norm[None, :] - 2.0 * gram
        kernel = jnp.exp(-0.5 * dist).astype(jnp.bfloat16)
        return jnp.dot(kernel, probes, preferred_element_type=jnp.float32)

    product = lax.map(one_block, jnp.arange(blocks, dtype=jnp.int32)).reshape(total, -1)
    return product + noise[:, None] * probes.astype(jnp.float32)
```

```python
import math

import jax
import jax.numpy as jnp
from jax import lax
from jax.experimental import pallas as pl
from jax.experimental.pallas import tpu as pltpu
from jax.sharding import PartitionSpec as P

ROOT_LOG2E = math.sqrt(math.log2(math.e))
NT = (((1,), (1,)), ((), ()))
LANES = 128
HALF = 64


def split_scaled(embeddings, inv_length):
    scaled = (embeddings * inv_length[None, :]) * ROOT_LOG2E
    high = lax.reduce_precision(scaled, 8, 7)
    return jnp.concatenate([high, scaled - high], axis=1).astype(jnp.bfloat16)


def augment(pair, is_col):
    count = pair.shape[0]
    wide = pair.astype(jnp.float32)
    swapped = pltpu.roll(wide, HALF, 1)
    whole = wide + swapped
    norm = jnp.sum(whole * whole, axis=1, keepdims=True) * -0.25
    first = norm.astype(jnp.bfloat16).astype(jnp.float32)
    rest = norm - first
    second = rest.astype(jnp.bfloat16).astype(jnp.float32)
    third = rest - second
    lane = lax.broadcasted_iota(jnp.int32, (count, LANES), 1)
    at, ones = (HALF + 3, HALF) if is_col else (HALF, HALF + 3)
    extra = jnp.where((lane >= ones) & (lane < ones + 3), 1.0, 0.0)
    extra = jnp.where(lane == at, first, extra)
    extra = jnp.where(lane == at + 1, second, extra)
    extra = jnp.where(lane == at + 2, third, extra)
    low = lane < HALF
    if is_col:
        left, right = jnp.where(low, wide, swapped), jnp.where(low, swapped, extra)
    else:
        left, right = wide, jnp.where(low, wide, extra)
    return left.astype(jnp.bfloat16), right.astype(jnp.bfloat16)


def tile_kernel(block, row_step):
    def body(row_ref, mine_ref, other_ref, out_ref, left, right, probes):
        rows = row_ref.shape[0] * row_ref.shape[1]
        groups = mine_ref.shape[0]

        def fill_rows(i, carry):
            a, b = augment(row_ref[i], False)
            at = pl.ds(pl.multiple_of(i * block, block), block)
            left[at, :LANES] = a
            left[at, LANES:] = b
            return carry

        lax.fori_loop(0, row_ref.shape[0], fill_rows, 0)
        per = 4
        for half, src in enumerate((mine_ref, other_ref)):
            for start in range(0, groups, per):
                def fill_cols(i, carry):
                    a, b = augment(src[start + i, :, :LANES], True)
                    at = pl.ds(pl.multiple_of(i * block, block), block)
                    right[at, :LANES] = a
                    right[at, LANES:] = b
                    probes[at, :] = src[start + i, :, LANES:]
                    return carry

                lax.fori_loop(0, per, fill_cols, 0)
                first = half == 0 and start == 0

                def step(i, carry):
                    at = pl.ds(pl.multiple_of(i * row_step, row_step), row_step)
                    gram = lax.dot_general(left[at, :], right[...], NT, preferred_element_type=jnp.float32)
                    kernel = jnp.exp2(gram).astype(jnp.bfloat16)
                    part = jnp.dot(kernel, probes[...], preferred_element_type=jnp.float32)
                    if first:
                        out_ref[at, :] = part
                    else:
                        out_ref[at, :] += part
                    return carry

                lax.fori_loop(0, rows // row_step, step, 0)

    return body


def tile_product(rows, mine, other):
    block = rows.shape[1]
    count = rows.shape[0] * block
    width = mine.shape[2] - LANES
    cols = 4 * block
    vmem = pl.BlockSpec(memory_space=pltpu.VMEM)
    return pl.pallas_call(
        tile_kernel(block, 1024),
        in_specs=[vmem] * 3,
        out_specs=vmem,
        out_shape=jax.ShapeDtypeStruct((count, width), jnp.float32),
        scratch_shapes=[
            pltpu.VMEM((count, 2 * LANES), jnp.bfloat16),
            pltpu.VMEM((cols, 2 * LANES), jnp.bfloat16),
            pltpu.VMEM((cols, width), jnp.bfloat16),
        ],
        compiler_params=pltpu.CompilerParams(vmem_limit_bytes=56 << 20),
        name="tile_product",
    )(rows, mine, other)


def solution(mesh):
    row_size, col_size = mesh.shape["row"], mesh.shape["col"]
    same_core = [list(range(core, row_size, 2)) for core in range(2)]
    chips = row_size // 2

    def on_device(embeddings, inv_length, noise, probes):
        block, width = probes.shape
        pair = split_scaled(embeddings, inv_length)
        packed = jnp.concatenate([pair, probes], axis=1)
        rows = lax.all_to_all(jnp.broadcast_to(pair[None], (col_size, *pair.shape)), "col", 0, 0)
        mine = lax.all_to_all(
            jnp.broadcast_to(packed[None], (chips, *packed.shape)), "row", 0, 0, axis_index_groups=same_core
        )
        other = lax.ppermute(mine, "row", [(i, i ^ 1) for i in range(row_size)])
        partial = tile_product(rows, mine, other)
        sent = partial.reshape(col_size, block, width).astype(jnp.bfloat16)
        got = lax.all_to_all(sent, "col", 0, 0)
        return jnp.sum(got.astype(jnp.float32), axis=0) + noise[:, None] * probes.astype(jnp.float32)

    return jax.shard_map(
        on_device,
        mesh=mesh,
        in_specs=(P(("row", "col"), None), P(), P(("row", "col")), P(("row", "col"), None)),
        out_specs=P(("row", "col"), None),
        check_vma=False,
    )
```

```python
import math

import jax
import jax.numpy as jnp
from jax import lax
from jax.experimental import pallas as pl
from jax.experimental.pallas import tpu as pltpu
from jax.sharding import PartitionSpec as P


ROOT_LOG2E = math.sqrt(math.log2(math.e))
NT = (((1,), (1,)), ((), ()))
LANES = 128
HALF = 64
AXES = ("row", "col")
VMEM = pl.BlockSpec(memory_space=pltpu.VMEM)


def place(x, y, z, core):
    return ((y % 2) * 8 + x * 2 + core) * 8 + (y // 2) * 4 + z


def fetch(value, dx=0, dy=0, dz=0, dcore=0):
    pairs = [
        (place((x + dx) % 4, (y + dy) % 4, (z + dz) % 4, core ^ dcore), place(x, y, z, core))
        for x in range(4)
        for y in range(4)
        for z in range(4)
        for core in range(2)
    ]
    return lax.ppermute(value, AXES, pairs)


def split_scaled(embeddings, inv_length):
    scaled = (embeddings * inv_length[None, :]) * ROOT_LOG2E
    high = lax.reduce_precision(scaled, 8, 7)
    return jnp.concatenate([high, scaled - high], axis=1).astype(jnp.bfloat16)


def augment(pair, is_col):
    count = pair.shape[0]
    wide = pair.astype(jnp.float32)
    swapped = pltpu.roll(wide, HALF, 1)
    whole = wide + swapped
    norm = jnp.sum(whole * whole, axis=1, keepdims=True) * -0.25
    first = norm.astype(jnp.bfloat16).astype(jnp.float32)
    rest = norm - first
    second = rest.astype(jnp.bfloat16).astype(jnp.float32)
    third = rest - second
    lane = lax.broadcasted_iota(jnp.int32, (count, LANES), 1)
    at, ones = (HALF + 3, HALF) if is_col else (HALF, HALF + 3)
    extra = jnp.where((lane >= ones) & (lane < ones + 3), 1.0, 0.0)
    extra = jnp.where(lane == at, first, extra)
    extra = jnp.where(lane == at + 1, second, extra)
    extra = jnp.where(lane == at + 2, third, extra)
    low = lane < HALF
    if is_col:
        left, right = jnp.where(low, wide, swapped), jnp.where(low, swapped, extra)
    else:
        left, right = wide, jnp.where(low, wide, extra)
    return left.astype(jnp.bfloat16), right.astype(jnp.bfloat16)


def prepare_rows(pairs):
    flat = [p for group in pairs for p in group]
    block = flat[0].shape[0]

    def body(*refs):
        ins, outs = iter(refs[: len(flat)]), refs[len(flat) :]
        for group, out in zip(pairs, outs, strict=True):
            for i in range(len(group)):
                a, b = augment(next(ins)[...], False)
                out[i * block : (i + 1) * block, :LANES] = a
                out[i * block : (i + 1) * block, LANES:] = b

    return pl.pallas_call(
        body,
        in_specs=[VMEM] * len(flat),
        out_specs=[VMEM] * len(pairs),
        out_shape=[jax.ShapeDtypeStruct((len(g) * block, 2 * LANES), jnp.bfloat16) for g in pairs],
        compiler_params=pltpu.CompilerParams(vmem_limit_bytes=12 << 20),
        name="prepare_rows",
    )(*flat)


def accumulate(rows, totals, blocks, steps, name):
    block = blocks[0].shape[0]
    width = blocks[0].shape[1] - LANES
    n, cols = len(rows), len(blocks) * block
    olds = list(totals) if totals is not None else []

    def body(*refs):
        row_refs, old_refs = refs[:n], refs[n : n + len(olds)]
        block_refs = refs[n + len(olds) : n + len(olds) + len(blocks)]
        out_refs = refs[n + len(olds) + len(blocks) : -2]
        right, probes = refs[-2:]
        for i, src in enumerate(block_refs):
            a, b = augment(src[:, :LANES], True)
            right[i * block : (i + 1) * block, :LANES] = a
            right[i * block : (i + 1) * block, LANES:] = b
            probes[i * block : (i + 1) * block, :] = src[:, LANES:]
        for k in range(n):
            step = steps[k]

            def one(i, carry):
                at = pl.ds(pl.multiple_of(i * step, step), step)
                gram = lax.dot_general(row_refs[k][at, :], right[...], NT, preferred_element_type=jnp.float32)
                kernel = jnp.exp2(gram).astype(jnp.bfloat16)
                part = jnp.dot(kernel, probes[...], preferred_element_type=jnp.float32)
                out_refs[k][at, :] = old_refs[k][at, :] + part if olds else part
                return carry

            lax.fori_loop(0, rows[k].shape[0] // step, one, 0)

    total = sum(r.shape[0] for r in rows)
    return pl.pallas_call(
        body,
        in_specs=[VMEM] * (n + len(olds) + len(blocks)),
        out_specs=[VMEM] * n,
        out_shape=[jax.ShapeDtypeStruct((r.shape[0], width), jnp.float32) for r in rows],
        scratch_shapes=[pltpu.VMEM((cols, 2 * LANES), jnp.bfloat16), pltpu.VMEM((cols, width), jnp.bfloat16)],
        input_output_aliases={n + i: i for i in range(len(olds))},
        cost_estimate=pl.CostEstimate(
            flops=4 * total * cols * 2 * LANES, transcendentals=total * cols, bytes_accessed=4 * total * width
        ),
        compiler_params=pltpu.CompilerParams(vmem_limit_bytes=36 << 20),
        name=name,
    )(*rows, *olds, *blocks)


def on_device(embeddings, inv_length, noise, probes):
    block = probes.shape[0]
    pair = split_scaled(embeddings, inv_length)
    own = jnp.concatenate([pair, probes], axis=1)

    east, west = fetch(own, dx=1), fetch(own, dx=-1)
    north, south = fetch(own, dy=1), fetch(own, dy=-1)

    up, down, far = fetch(pair, dz=1), fetch(pair, dz=-1), fetch(pair, dz=2)
    across = [fetch(p, dcore=1) for p in (pair, up, down, far)]
    row_far, row_near, row_own = prepare_rows([across, [up, down, far], [pair]])

    ne, sw = fetch(north, dx=1), fetch(south, dx=-1)
    nw, se = fetch(west, dy=1), fetch(east, dy=-1)
    first = [own, east, west, north, south]
    far_sum, near_sum = accumulate([row_far, row_near], None, first, (768, 1152), "round1")

    een, wws = fetch(ne, dx=1), fetch(sw, dx=-1)
    nnw, sse = fetch(nw, dy=1), fetch(se, dy=-1)
    second = [ne, sw, nw, se]
    far_sum, near_sum = accumulate([row_far, row_near], (far_sum, near_sum), second, (768, 1152), "round2")

    ee, nn, corner = fetch(east, dx=1), fetch(north, dy=1), fetch(nnw, dx=-1)
    third = [een, wws, nnw, sse]
    far_sum, near_sum = accumulate([row_far, row_near], (far_sum, near_sum), third, (768, 1152), "round3")

    fourth = [ee, nn, corner]
    (far_sum,) = accumulate([row_far], (far_sum,), fourth, (768,), "round4_far")
    got = fetch(far_sum, dcore=1)
    (near_sum,) = accumulate([row_near], (near_sum,), fourth, (1152,), "round4_near")
    sent = (near_sum + got[block:]).astype(jnp.bfloat16)
    back = [
        fetch(sent[:block], dz=-1),
        fetch(sent[block : 2 * block], dz=1),
        fetch(sent[2 * block :], dz=2),
    ]
    (own_sum,) = accumulate([row_own], None, first + second + third + fourth, (384,), "own_rows")
    result = own_sum + got[:block] + noise[:, None] * probes.astype(jnp.float32)
    for part in back:
        result = result + part.astype(jnp.float32)
    return result


def solution(mesh):
    return jax.shard_map(
        on_device,
        mesh=mesh,
        in_specs=(P(("row", "col"), None), P(), P(("row", "col")), P(("row", "col"), None)),
        out_specs=P(("row", "col"), None),
        check_vma=False,
    )
```

```python
import math

import jax
import jax.numpy as jnp
from jax import lax
from jax.experimental import pallas as pl
from jax.experimental.pallas import tpu as pltpu
from jax.sharding import PartitionSpec as P


ROOT_LOG2E = math.sqrt(math.log2(math.e))
NT = (((1,), (1,)), ((), ()))
LANES = 128
HALF = 64
AXES = ("row", "col")
VMEM = pl.BlockSpec(memory_space=pltpu.VMEM)


def place(x, y, z, core):
    return ((y % 2) * 8 + x * 2 + core) * 8 + (y // 2) * 4 + z


def swap(value, axes, flip):
    flips = flip if isinstance(flip, tuple) else (flip, flip)
    pairs = []
    for x in range(4):
        for y in range(4):
            for z in range(4):
                for core in range(2):
                    to = {"x": x, "y": y, "z": z}
                    to[axes[core]] ^= flips[core]
                    pairs.append((place(x, y, z, core), place(to["x"], to["y"], to["z"], core)))
    return lax.ppermute(value, AXES, pairs)


def partner(value):
    return lax.ppermute(value, AXES, [(i, i ^ 8) for i in range(128)])


def augment(pair, is_col):
    count = pair.shape[0]
    wide = pair.astype(jnp.float32)
    swapped = pltpu.roll(wide, HALF, 1)
    whole = wide + swapped
    norm = jnp.sum(whole * whole, axis=1, keepdims=True) * -0.25
    first = norm.astype(jnp.bfloat16).astype(jnp.float32)
    rest = norm - first
    second = rest.astype(jnp.bfloat16).astype(jnp.float32)
    third = rest - second
    lane = lax.broadcasted_iota(jnp.int32, (count, LANES), 1)
    at, ones = (HALF + 3, HALF) if is_col else (HALF, HALF + 3)
    extra = jnp.where((lane >= ones) & (lane < ones + 3), 1.0, 0.0)
    extra = jnp.where(lane == at, first, extra)
    extra = jnp.where(lane == at + 1, second, extra)
    extra = jnp.where(lane == at + 2, third, extra)
    low = lane < HALF
    if is_col:
        return pair, jnp.where(low, wide, extra).astype(jnp.bfloat16)
    return jnp.where(low, wide, swapped).astype(jnp.bfloat16), jnp.where(low, swapped, extra).astype(jnp.bfloat16)


def pack_own(embeddings_t, inv_length, probes):
    block, width = probes.shape

    def body(emb_hbm, inv_hbm, probe_hbm, own_ref, pair_ref, emb_ref, inv_ref, sems):
        copies = [
            pltpu.make_async_copy(emb_hbm, emb_ref, sems.at[0]),
            pltpu.make_async_copy(inv_hbm, inv_ref, sems.at[1]),
            pltpu.make_async_copy(probe_hbm, own_ref.at[:, LANES:], sems.at[2]),
        ]
        for copy in copies:
            copy.start()
        copies[0].wait()
        copies[1].wait()
        emb = emb_ref[...]
        twice = jnp.concatenate([emb, emb], axis=0).T
        inv = inv_ref[...]
        scaled = (twice * jnp.concatenate([inv, inv], axis=1)) * ROOT_LOG2E
        high = scaled.astype(jnp.bfloat16).astype(jnp.float32)
        lane = lax.broadcasted_iota(jnp.int32, (block, LANES), 1)
        pair = jnp.where(lane < HALF, high, scaled - high).astype(jnp.bfloat16)
        pair_ref[...] = pair
        own_ref[:, :LANES] = pair
        copies[2].wait()

    return pl.pallas_call(
        body,
        in_specs=[pl.BlockSpec(memory_space=pltpu.HBM)] * 3,
        out_specs=[VMEM] * 2,
        out_shape=[
            jax.ShapeDtypeStruct((block, LANES + width), jnp.bfloat16),
            jax.ShapeDtypeStruct((block, LANES), jnp.bfloat16),
        ],
        scratch_shapes=[
            pltpu.VMEM(embeddings_t.shape, jnp.float32),
            pltpu.VMEM(inv_length.shape, jnp.float32),
            pltpu.SemaphoreType.DMA((3,)),
        ],
        compiler_params=pltpu.CompilerParams(vmem_limit_bytes=8 << 20),
        name="pack_own",
    )(embeddings_t, inv_length, probes)


def join(a, b):
    def body(a_ref, b_ref, out_ref):
        out_ref[: a.shape[0], :] = a_ref[...]
        out_ref[a.shape[0] :, :] = b_ref[...]

    return pl.pallas_call(
        body,
        in_specs=[VMEM] * 2,
        out_specs=VMEM,
        out_shape=jax.ShapeDtypeStruct((a.shape[0] + b.shape[0], a.shape[1]), a.dtype),
        compiler_params=pltpu.CompilerParams(vmem_limit_bytes=8 << 20),
    )(a, b)


def prepare_rows(block, sources, groups):
    def body(*refs):
        ins, outs = refs[: len(sources)], refs[len(sources) :]
        for group, out in zip(groups, outs, strict=True):
            for i, (source, k) in enumerate(group):
                a, b = augment(ins[source][k * block : (k + 1) * block, :], False)
                out[i * block : (i + 1) * block, :LANES] = a
                out[i * block : (i + 1) * block, LANES:] = b

    return pl.pallas_call(
        body,
        in_specs=[VMEM] * len(sources),
        out_specs=[VMEM] * len(groups),
        out_shape=[jax.ShapeDtypeStruct((len(g) * block, 2 * LANES), jnp.bfloat16) for g in groups],
        compiler_params=pltpu.CompilerParams(vmem_limit_bytes=12 << 20),
        name="prepare_rows",
    )(*sources)


def params(mib):
    return pltpu.CompilerParams(vmem_limit_bytes=mib << 20)


def cost(rows, cols, width):
    return pl.CostEstimate(
        flops=4 * rows * cols * 2 * LANES, transcendentals=rows * cols, bytes_accessed=4 * rows * width
    )


def fold(row_ref, at, column, probe):
    gram = lax.dot_general(row_ref[at, :], column, NT, preferred_element_type=jnp.float32)
    return jnp.dot(jnp.exp2(gram).astype(jnp.bfloat16), probe, preferred_element_type=jnp.float32)


def accumulate(rows, olds, packs, steps):
    block = 384
    width = packs[0].shape[1] - LANES
    n, m, p = len(rows), len(olds), len(packs)
    cols = sum(q.shape[0] for q in packs)

    def body(*refs):
        row_refs, old_refs, pack_refs = refs[:n], refs[n : n + m], refs[n + m : n + m + p]
        out_refs, (right, probes) = refs[n + m + p : -2], refs[-2:]
        start = 0
        for src in pack_refs:
            for k in range(0, src.shape[0], block):
                a, b = augment(src[k : k + block, :LANES], True)
                right[start : start + block, :LANES] = a
                right[start : start + block, LANES:] = b
                probes[start : start + block, :] = src[k : k + block, LANES:]
                start += block
        for k in range(n):
            step = steps[k]

            def one(i, carry):
                at = pl.ds(pl.multiple_of(i * step, step), step)
                part = fold(row_refs[k], at, right[...], probes[...])
                out_refs[k][at, :] = old_refs[k][at, :] + part if m else part
                return carry

            lax.fori_loop(0, rows[k].shape[0] // step, one, 0)

    return pl.pallas_call(
        body,
        in_specs=[VMEM] * (n + m + p),
        out_specs=[VMEM] * (n + 2),
        out_shape=[jax.ShapeDtypeStruct((r.shape[0], width), jnp.float32) for r in rows]
        + [jax.ShapeDtypeStruct((cols, 2 * LANES), jnp.bfloat16), jax.ShapeDtypeStruct((cols, width), jnp.bfloat16)],
        input_output_aliases={n + i: i for i in range(m)},
        cost_estimate=cost(sum(r.shape[0] for r in rows), cols, width),
        compiler_params=params(28),
    )(*rows, *olds, *packs)


def apply_rows(rows, old, columns, step):
    count, width = rows.shape[0], columns[0][1].shape[1]
    flat = [a for pair in columns for a in pair]
    lead = [rows] if old is None else [rows, old]

    def body(*refs):
        row_ref, out_ref, rest = refs[0], refs[-1], refs[len(lead) : -1]

        def one(i, carry):
            at = pl.ds(pl.multiple_of(i * step, step), step)
            part = None if old is None else refs[1][at, :]
            for k in range(0, len(rest), 2):
                more = fold(row_ref, at, rest[k][...], rest[k + 1][...])
                part = more if part is None else part + more
            out_ref[at, :] = part
            return carry

        lax.fori_loop(0, count // step, one, 0)

    return pl.pallas_call(
        body,
        in_specs=[VMEM] * (len(lead) + len(flat)),
        out_specs=VMEM,
        out_shape=jax.ShapeDtypeStruct((count, width), jnp.float32),
        input_output_aliases={} if old is None else {1: 0},
        cost_estimate=cost(count, sum(c[0].shape[0] for c in columns), width),
        compiler_params=params(28),
    )(*lead, *flat)


def on_device(embeddings, inv_length, noise, probes):
    block = probes.shape[0]
    own, pair = pack_own(embeddings.T, inv_length[None, :], probes)

    first_axis, second_axis = ("x", "y"), ("y", "x")
    beside = swap(own, first_axis, 1)
    rows_a = swap(pair, "zz", (1, 3))
    pairs = join(pair, rows_a)
    rows_b = swap(pairs, "zz", (3, 1))
    pack_a = join(own, beside)
    pack_b = swap(pack_a, first_axis, 3)
    pack_c = swap(pack_a, second_axis, 1)
    pack_d = swap(pack_a, second_axis, 3)
    other_pairs = partner(pairs)
    other_b = partner(rows_b)
    row_far, row_near, row_own = prepare_rows(
        block,
        [pairs, rows_b, other_pairs, other_b],
        [[(2, 0), (2, 1), (3, 1), (3, 0)], [(0, 1), (1, 1), (1, 0)], [(0, 0)]],
    )
    rows, steps = [row_far, row_near], (768, 1152)
    far, near, right_a, probes_a = accumulate(rows, [], [pack_a], steps)

    pack_e = swap(pack_b, second_axis, 1)
    pack_f = swap(pack_b, second_axis, 3)
    pack_g = swap(pack_d, second_axis, 1)
    far, near, right_b, probes_b = accumulate(rows, [far, near], [pack_b, pack_c], steps)

    pack_h = swap(pack_e, second_axis, 3)
    far, near, right_c, probes_c = accumulate(rows, [far, near], [pack_d, pack_e], steps)

    last = [pack_f, pack_g, pack_h]
    far, right_d, probes_d = accumulate([row_far], [far], last, (768,))
    got = partner(far)
    near = apply_rows(row_near, near, [(right_d, probes_d)], 1152)
    sums = near + got[block:]
    in_a = swap(sums[: 2 * block].astype(jnp.bfloat16), "zz", (1, 3))
    columns = [(right_a, probes_a), (right_b, probes_b), (right_c, probes_c), (right_d, probes_d)]
    own_sum = apply_rows(row_own, None, columns, 384)
    passed = (sums[2 * block :] + in_a[block:].astype(jnp.float32)).astype(jnp.bfloat16)
    in_b = swap(passed, "zz", (3, 1))
    result = own_sum + got[:block] + noise[:, None] * probes.astype(jnp.float32)
    return result + in_a[:block].astype(jnp.float32) + in_b.astype(jnp.float32)


def solution(mesh):
    return jax.shard_map(
        on_device,
        mesh=mesh,
        in_specs=(P(("row", "col"), None), P(), P(("row", "col")), P(("row", "col"), None)),
        out_specs=P(("row", "col"), None),
        check_vma=False,
    )
```

```python
import math

import jax
import jax.numpy as jnp
from jax import lax
from jax.experimental import pallas as pl
from jax.experimental.pallas import tpu as pltpu
from jax.sharding import PartitionSpec as P


ROOT_LOG2E = math.sqrt(math.log2(math.e))
NT = (((1,), (1,)), ((), ()))
LANES = 128
HALF = 64
AXES = ("row", "col")
VMEM = pl.BlockSpec(memory_space=pltpu.VMEM)


def place(x, y, z, core):
    return ((y % 2) * 8 + x * 2 + core) * 8 + (y // 2) * 4 + z


def swap(value, moves):
    pairs = []
    for x in range(4):
        for y in range(4):
            for z in range(4):
                for core, (axis, flip) in enumerate(moves):
                    to = {"x": x, "y": y, "z": z}
                    to[axis] ^= flip
                    pairs.append((place(x, y, z, core), place(to["x"], to["y"], to["z"], core)))
    return lax.ppermute(value, AXES, pairs)


def partner(value):
    return lax.ppermute(value, AXES, [(i, i ^ 8) for i in range(128)])


def augment(pair, is_col):
    count = pair.shape[0]
    wide = pair.astype(jnp.float32)
    swapped = pltpu.roll(wide, HALF, 1)
    whole = wide + swapped
    norm = jnp.sum(whole * whole, axis=1, keepdims=True) * -0.25
    first = norm.astype(jnp.bfloat16).astype(jnp.float32)
    rest = norm - first
    second = rest.astype(jnp.bfloat16).astype(jnp.float32)
    third = rest - second
    lane = lax.broadcasted_iota(jnp.int32, (count, LANES), 1)
    at, ones = (HALF + 3, HALF) if is_col else (HALF, HALF + 3)
    extra = jnp.where((lane >= ones) & (lane < ones + 3), 1.0, 0.0)
    extra = jnp.where(lane == at, first, extra)
    extra = jnp.where(lane == at + 1, second, extra)
    extra = jnp.where(lane == at + 2, third, extra)
    low = lane < HALF
    if is_col:
        return pair, jnp.where(low, wide, extra).astype(jnp.bfloat16)
    return jnp.where(low, wide, swapped).astype(jnp.bfloat16), jnp.where(low, swapped, extra).astype(jnp.bfloat16)


def pack_own(embeddings_t, inv_length, probes):
    block, width = probes.shape

    def body(emb_hbm, inv_hbm, probe_hbm, own_ref, pair_ref, emb_ref, inv_ref, sems):
        copies = [
            pltpu.make_async_copy(emb_hbm, emb_ref, sems.at[0]),
            pltpu.make_async_copy(inv_hbm, inv_ref, sems.at[1]),
            pltpu.make_async_copy(probe_hbm, own_ref.at[:, LANES:], sems.at[2]),
        ]
        for copy in copies:
            copy.start()
        copies[0].wait()
        copies[1].wait()
        emb = emb_ref[...]
        twice = jnp.concatenate([emb, emb], axis=0).T
        inv = inv_ref[...]
        scaled = (twice * jnp.concatenate([inv, inv], axis=1)) * ROOT_LOG2E
        high = scaled.astype(jnp.bfloat16).astype(jnp.float32)
        lane = lax.broadcasted_iota(jnp.int32, (block, LANES), 1)
        pair = jnp.where(lane < HALF, high, scaled - high).astype(jnp.bfloat16)
        pair_ref[...] = pair
        own_ref[:, :LANES] = pair
        copies[2].wait()

    return pl.pallas_call(
        body,
        in_specs=[pl.BlockSpec(memory_space=pltpu.HBM)] * 3,
        out_specs=[VMEM] * 2,
        out_shape=[
            jax.ShapeDtypeStruct((block, LANES + width), jnp.bfloat16),
            jax.ShapeDtypeStruct((block, LANES), jnp.bfloat16),
        ],
        scratch_shapes=[
            pltpu.VMEM(embeddings_t.shape, jnp.float32),
            pltpu.VMEM(inv_length.shape, jnp.float32),
            pltpu.SemaphoreType.DMA((3,)),
        ],
        compiler_params=pltpu.CompilerParams(vmem_limit_bytes=64900 << 10),
        name="pack_own",
    )(embeddings_t, inv_length, probes)


def join(a, b):
    def body(a_ref, b_ref, out_ref):
        out_ref[: a.shape[0], :] = a_ref[...]
        out_ref[a.shape[0] :, :] = b_ref[...]

    return pl.pallas_call(
        body,
        in_specs=[VMEM] * 2,
        out_specs=VMEM,
        out_shape=jax.ShapeDtypeStruct((a.shape[0] + b.shape[0], a.shape[1]), a.dtype),
        compiler_params=pltpu.CompilerParams(vmem_limit_bytes=8 << 20),
    )(a, b)


def prepare_rows(block, sources, groups):
    def body(*refs):
        ins, outs = refs[: len(sources)], refs[len(sources) :]
        for group, out in zip(groups, outs, strict=True):
            for i, (source, k) in enumerate(group):
                a, b = augment(ins[source][k * block : (k + 1) * block, :], False)
                out[i * block : (i + 1) * block, :LANES] = a
                out[i * block : (i + 1) * block, LANES:] = b

    return pl.pallas_call(
        body,
        in_specs=[VMEM] * len(sources),
        out_specs=[VMEM] * len(groups),
        out_shape=[jax.ShapeDtypeStruct((len(g) * block, 2 * LANES), jnp.bfloat16) for g in groups],
        compiler_params=pltpu.CompilerParams(vmem_limit_bytes=12 << 20),
        name="prepare_rows",
    )(*sources)


def params(mib):
    return pltpu.CompilerParams(vmem_limit_bytes=mib << 20)


def cost(rows, cols, width):
    return pl.CostEstimate(
        flops=4 * rows * cols * 2 * LANES, transcendentals=rows * cols, bytes_accessed=4 * rows * width
    )


def fold(row_ref, at, column, probe):
    gram = lax.dot_general(row_ref[at, :], column, NT, preferred_element_type=jnp.float32)
    return jnp.dot(jnp.exp2(gram).astype(jnp.bfloat16), probe, preferred_element_type=jnp.float32)


def accumulate(rows, olds, packs, out_types):
    n, m, p = len(rows), len(olds), len(packs)
    width = packs[0].shape[1] - LANES
    cols = sum(q.shape[0] for q in packs)
    block = 384

    def body(*refs):
        row_refs, old_refs, pack_refs = refs[:n], refs[n : n + m], refs[n + m : n + m + p]
        out_refs, (right, probes) = refs[n + m + p : -2], refs[-2:]
        start = 0
        for src in pack_refs:
            for k in range(0, src.shape[0], block):
                a, b = augment(src[k : k + block, :LANES], True)
                right[start : start + block, :LANES] = a
                right[start : start + block, LANES:] = b
                probes[start : start + block, :] = src[k : k + block, LANES:]
                start += block
        for k in range(n):
            part = fold(row_refs[k], slice(None), right[...], probes[...])
            out_refs[k][...] = (old_refs[k][...] + part if m else part).astype(out_refs[k].dtype)

    return pl.pallas_call(
        body,
        in_specs=[VMEM] * (n + m + p),
        out_specs=[VMEM] * (n + 2),
        out_shape=[jax.ShapeDtypeStruct((r.shape[0], width), t) for r, t in zip(rows, out_types, strict=True)]
        + [jax.ShapeDtypeStruct((cols, 2 * LANES), jnp.bfloat16), jax.ShapeDtypeStruct((cols, width), jnp.bfloat16)],
        cost_estimate=cost(sum(r.shape[0] for r in rows), cols, width),
        compiler_params=params(28),
    )(*rows, *olds, *packs)


def apply_rows(rows, first_row, count, old, columns, out_type):
    width = columns[0][1].shape[1]
    flat = [a for pair in columns for a in pair]
    lead = [rows] if old is None else [rows, old]

    def body(*refs):
        row_ref, out_ref, rest = refs[0], refs[-1], refs[len(lead) : -1]
        part = None if old is None else refs[1][...]
        for k in range(0, len(rest), 2):
            more = fold(row_ref, pl.ds(first_row, count), rest[k][...], rest[k + 1][...])
            part = more if part is None else part + more
        out_ref[...] = part.astype(out_type)

    return pl.pallas_call(
        body,
        in_specs=[VMEM] * (len(lead) + len(flat)),
        out_specs=VMEM,
        out_shape=jax.ShapeDtypeStruct((count, width), out_type),
        cost_estimate=cost(count, sum(c[0].shape[0] for c in columns), width),
        compiler_params=params(28),
    )(*lead, *flat)


COL_MOVES = ((("x", 1), ("x", 3)), (("x", 3), ("y", 1)), (("y", 1), ("x", 1)))
ROW_MOVES = ((("z", 1), ("z", 3)), (("z", 3), ("y", 3)), (("y", 3), ("z", 1)))


def on_device(embeddings, inv_length, noise, probes):
    block = probes.shape[0]
    two = 2 * block
    f32, bf16 = jnp.float32, jnp.bfloat16
    move_a, move_b, move_c = COL_MOVES
    move_p, move_q, move_r = ROW_MOVES
    own, pair = pack_own(embeddings.T, inv_length[None, :], probes)

    got_a = swap(own, move_a)
    rows_p = swap(pair, move_p)
    pairs = join(pair, rows_p)
    rows_q = swap(pairs, move_q)
    pack_a = join(own, got_a)
    pack_b = swap(pack_a, move_b)
    pack_c = swap(pack_a, move_c)
    other_a = partner(pack_a)
    quads = join(pairs, rows_q)
    rows_r = swap(quads, move_r)
    row_f1, row_f2, row_n1, row_n2 = prepare_rows(
        block, [quads, rows_r], [[(1, 2), (1, 3)], [(1, 0), (1, 1)], [(0, 2), (0, 3)], [(0, 0), (0, 1)]]
    )
    far = [row_f1, row_f2]
    f1, f2, *aug_a = accumulate(far, [], [pack_a, other_a], [f32, f32])

    other_b, other_c = partner(pack_b), partner(pack_c)
    pack_d = swap(pack_b, move_c)
    f1, f2, *aug_b = accumulate(far, [f1, f2], [pack_b, other_b], [f32, f32])
    f1, f2, *aug_c = accumulate(far, [f1, f2], [pack_c, other_c], [f32, f32])
    other_d = partner(pack_d)
    n1 = apply_rows(row_n1, 0, two, None, [aug_a, aug_b], f32)
    f1, *aug_d = accumulate([row_f1], [f1], [pack_d, other_d], [bf16])
    in_1 = swap(f1, move_r)
    f2 = apply_rows(row_f2, 0, two, f2, [aug_d], bf16)
    in_2 = swap(f2, move_r)
    n1 = apply_rows(row_n1, 0, two, n1, [aug_c, aug_d], f32)
    in_3 = swap((n1 + in_1.astype(f32)).astype(bf16), move_q)
    columns = [aug_a, aug_b, aug_c, aug_d]
    beside = apply_rows(row_n2, block, block, None, columns, f32)
    passed = beside + in_2[block:].astype(f32) + in_3[block:].astype(f32)
    in_4 = swap(passed.astype(bf16), move_p)
    total = apply_rows(row_n2, 0, block, None, columns, f32)
    total = total + in_2[:block].astype(f32) + in_3[:block].astype(f32) + in_4.astype(f32)
    return total + noise[:, None] * probes.astype(f32)


def solution(mesh):
    return jax.shard_map(
        on_device,
        mesh=mesh,
        in_specs=(P(("row", "col"), None), P(), P(("row", "col")), P(("row", "col"), None)),
        out_specs=P(("row", "col"), None),
        check_vma=False,
    )
```

```python
import math

import jax
import jax.numpy as jnp
from jax import lax
from jax.experimental import pallas as pl
from jax.experimental.pallas import tpu as pltpu
from jax.sharding import PartitionSpec as P


ROOT_LOG2E = math.sqrt(math.log2(math.e))
NT = (((1,), (1,)), ((), ()))
LANES = 128
HALF = 64
AXES = ("row", "col")
VMEM = pl.BlockSpec(memory_space=pltpu.VMEM)


def place(x, y, z, core):
    return ((y % 2) * 8 + x * 2 + core) * 8 + (y // 2) * 4 + z


def swap(value, moves):
    pairs = []
    for x in range(4):
        for y in range(4):
            for z in range(4):
                for core, (axis, flip) in enumerate(moves):
                    to = {"x": x, "y": y, "z": z}
                    to[axis] ^= flip
                    pairs.append((place(x, y, z, core), place(to["x"], to["y"], to["z"], core)))
    return lax.ppermute(value, AXES, pairs)


def partner(value):
    return lax.ppermute(value, AXES, [(i, i ^ 8) for i in range(128)])


def augment(pair, is_col):
    count = pair.shape[0]
    wide = pair.astype(jnp.float32)
    swapped = pltpu.roll(wide, HALF, 1)
    whole = wide + swapped
    norm = jnp.sum(whole * whole, axis=1, keepdims=True) * -0.25
    first = norm.astype(jnp.bfloat16).astype(jnp.float32)
    rest = norm - first
    second = rest.astype(jnp.bfloat16).astype(jnp.float32)
    third = rest - second
    lane = lax.broadcasted_iota(jnp.int32, (count, LANES), 1)
    at, ones = (HALF + 3, HALF) if is_col else (HALF, HALF + 3)
    extra = jnp.where((lane >= ones) & (lane < ones + 3), 1.0, 0.0)
    extra = jnp.where(lane == at, first, extra)
    extra = jnp.where(lane == at + 1, second, extra)
    extra = jnp.where(lane == at + 2, third, extra)
    low = lane < HALF
    if is_col:
        return pair, jnp.where(low, wide, extra).astype(jnp.bfloat16)
    return jnp.where(low, wide, swapped).astype(jnp.bfloat16), jnp.where(low, swapped, extra).astype(jnp.bfloat16)


def pack_own(embeddings_t, inv_length, probes):
    block, width = probes.shape

    def body(emb_hbm, inv_hbm, probe_hbm, own_ref, pair_ref, emb_ref, inv_ref, sems):
        copies = [
            pltpu.make_async_copy(emb_hbm, emb_ref, sems.at[0]),
            pltpu.make_async_copy(inv_hbm, inv_ref, sems.at[1]),
            pltpu.make_async_copy(probe_hbm, own_ref.at[:, LANES:], sems.at[2]),
        ]
        for copy in copies:
            copy.start()
        copies[0].wait()
        copies[1].wait()
        emb = emb_ref[...]
        twice = jnp.concatenate([emb, emb], axis=0).T
        inv = inv_ref[...]
        scaled = (twice * jnp.concatenate([inv, inv], axis=1)) * ROOT_LOG2E
        high = scaled.astype(jnp.bfloat16).astype(jnp.float32)
        lane = lax.broadcasted_iota(jnp.int32, (block, LANES), 1)
        pair = jnp.where(lane < HALF, high, scaled - high).astype(jnp.bfloat16)
        pair_ref[...] = pair
        own_ref[:, :LANES] = pair
        copies[2].wait()

    return pl.pallas_call(
        body,
        in_specs=[pl.BlockSpec(memory_space=pltpu.HBM)] * 3,
        out_specs=[VMEM] * 2,
        out_shape=[
            jax.ShapeDtypeStruct((block, LANES + width), jnp.bfloat16),
            jax.ShapeDtypeStruct((block, LANES), jnp.bfloat16),
        ],
        scratch_shapes=[
            pltpu.VMEM(embeddings_t.shape, jnp.float32),
            pltpu.VMEM(inv_length.shape, jnp.float32),
            pltpu.SemaphoreType.DMA((3,)),
        ],
        compiler_params=pltpu.CompilerParams(vmem_limit_bytes=64900 << 10),
        name="pack_own",
    )(embeddings_t, inv_length, probes)


def join(a, b):
    width = b.shape[1]

    def body(a_ref, b_ref, out_ref):
        out_ref[: a.shape[0], :] = a_ref[:, :width]
        out_ref[a.shape[0] :, :] = b_ref[...]

    return pl.pallas_call(
        body,
        in_specs=[VMEM] * 2,
        out_specs=VMEM,
        out_shape=jax.ShapeDtypeStruct((a.shape[0] + b.shape[0], width), a.dtype),
        compiler_params=pltpu.CompilerParams(vmem_limit_bytes=8 << 20),
    )(a, b)


def prepare_rows(block, sources, groups):
    def body(*refs):
        ins, outs = refs[: len(sources)], refs[len(sources) :]
        for group, out in zip(groups, outs, strict=True):
            for i, (source, k) in enumerate(group):
                a, b = augment(ins[source][k * block : (k + 1) * block, :], False)
                out[i * block : (i + 1) * block, :LANES] = a
                out[i * block : (i + 1) * block, LANES:] = b

    return pl.pallas_call(
        body,
        in_specs=[VMEM] * len(sources),
        out_specs=[VMEM] * len(groups),
        out_shape=[jax.ShapeDtypeStruct((len(g) * block, 2 * LANES), jnp.bfloat16) for g in groups],
        compiler_params=pltpu.CompilerParams(vmem_limit_bytes=12 << 20),
    )(*sources)


def params(mib):
    return pltpu.CompilerParams(vmem_limit_bytes=mib << 20)


def cost(rows, cols, width):
    return pl.CostEstimate(
        flops=4 * rows * cols * 2 * LANES, transcendentals=rows * cols, bytes_accessed=4 * rows * width
    )


def fold(row_ref, at, column, probe):
    gram = lax.dot_general(row_ref[at, :], column, NT, preferred_element_type=jnp.float32)
    return jnp.dot(jnp.exp2(gram).astype(jnp.bfloat16), probe, preferred_element_type=jnp.float32)


def accumulate(rows, olds, packs, out_types):
    n, m, p = len(rows), len(olds), len(packs)
    width = packs[0].shape[1] - LANES
    cols = sum(q.shape[0] for q in packs)
    block = 384

    def body(*refs):
        row_refs, old_refs, pack_refs = refs[:n], refs[n : n + m], refs[n + m : n + m + p]
        out_refs, (right, probes) = refs[n + m + p : -2], refs[-2:]
        start = 0
        for src in pack_refs:
            for k in range(0, src.shape[0], block):
                a, b = augment(src[k : k + block, :LANES], True)
                right[start : start + block, :LANES] = a
                right[start : start + block, LANES:] = b
                probes[start : start + block, :] = src[k : k + block, LANES:]
                start += block
        for k in range(n):
            part = fold(row_refs[k], slice(None), right[...], probes[...])
            out_refs[k][...] = (old_refs[k][...] + part if m else part).astype(out_refs[k].dtype)

    return pl.pallas_call(
        body,
        in_specs=[VMEM] * (n + m + p),
        out_specs=[VMEM] * (n + 2),
        out_shape=[jax.ShapeDtypeStruct((r.shape[0], width), t) for r, t in zip(rows, out_types, strict=True)]
        + [jax.ShapeDtypeStruct((cols, 2 * LANES), jnp.bfloat16), jax.ShapeDtypeStruct((cols, width), jnp.bfloat16)],
        cost_estimate=cost(sum(r.shape[0] for r in rows), cols, width),
        compiler_params=params(28),
    )(*rows, *olds, *packs)


def apply_rows(rows, old, columns, out_type):
    count, width = rows.shape[0], columns[0][1].shape[1]
    flat = [a for pair in columns for a in pair]
    lead = [rows] if old is None else [rows, old]

    def body(*refs):
        row_ref, out_ref, rest = refs[0], refs[-1], refs[len(lead) : -1]
        part = None if old is None else refs[1][...]
        for k in range(0, len(rest), 2):
            more = fold(row_ref, slice(None), rest[k][...], rest[k + 1][...])
            part = more if part is None else part + more
        out_ref[...] = part.astype(out_type)

    return pl.pallas_call(
        body,
        in_specs=[VMEM] * (len(lead) + len(flat)),
        out_specs=VMEM,
        out_shape=jax.ShapeDtypeStruct((count, width), out_type),
        cost_estimate=cost(count, sum(c[0].shape[0] for c in columns), width),
        compiler_params=params(28),
    )(*lead, *flat)


COL_MOVES = ((("x", 1), ("x", 3)), (("x", 3), ("y", 1)), (("y", 1), ("x", 1)))
ROW_MOVES = ((("z", 1), ("z", 3)), (("z", 3), ("y", 3)), (("y", 3), ("z", 1)))


def diagonal(noise, probes):
    return lax.optimization_barrier(noise[:, None] * probes.astype(jnp.float32))


def on_device(embeddings, inv_length, noise, probes):
    block = probes.shape[0]
    f32, bf16 = jnp.float32, jnp.bfloat16
    move_a, move_b, move_c = COL_MOVES
    move_p, move_q, move_r = ROW_MOVES
    own, pair = pack_own(embeddings.T, inv_length[None, :], probes)
    diag = diagonal(noise, probes)

    got_a = swap(own, move_a)
    rows_p = swap(pair, move_p)
    pairs = join(own, rows_p)
    rows_q = swap(pairs, move_q)
    pack_a = join(own, got_a)
    pack_b = swap(pack_a, move_b)
    pack_c = swap(pack_a, move_c)
    other_a = partner(pack_a)
    quads = join(pairs, rows_q)
    rows_r = swap(quads, move_r)

    near = prepare_rows(block, [quads], [[(0, 2), (0, 3)], [(0, 1)], [(0, 0)]])
    row_n, row_p, row_own = near
    n, beside, total, *aug_a = accumulate(near, [], [pack_a, other_a], [f32, f32, f32])

    other_b, other_c = partner(pack_b), partner(pack_c)
    pack_d = swap(pack_b, move_c)
    far = prepare_rows(block, [rows_r], [[(0, 2), (0, 3)], [(0, 0), (0, 1)]])
    f1 = apply_rows(far[0], None, [aug_a], f32)
    f2 = apply_rows(far[1], None, [aug_a], f32)
    f1, f2, *aug_b = accumulate(far, [f1, f2], [pack_b, other_b], [f32, f32])
    other_d = partner(pack_d)
    f1, f2, *aug_c = accumulate(far, [f1, f2], [pack_c, other_c], [f32, f32])
    f1, *aug_d = accumulate(far[:1], [f1], [pack_d, other_d], [bf16])
    in_1 = swap(f1, move_r)
    f2 = apply_rows(far[1], f2, [aug_d], bf16)
    in_2 = swap(f2, move_r)

    columns = [aug_b, aug_c, aug_d]
    n = apply_rows(row_n, n, columns, f32)
    in_3 = swap((n + in_1.astype(f32)).astype(bf16), move_q)
    beside = apply_rows(row_p, beside, columns, f32)
    passed = beside + in_2[block:].astype(f32) + in_3[block:].astype(f32)
    in_4 = swap(passed.astype(bf16), move_p)
    total = apply_rows(row_own, total, columns, f32)
    return total + diag + in_2[:block].astype(f32) + in_3[:block].astype(f32) + in_4.astype(f32)


def solution(mesh):
    return jax.shard_map(
        on_device,
        mesh=mesh,
        in_specs=(P(("row", "col"), None), P(), P(("row", "col")), P(("row", "col"), None)),
        out_specs=P(("row", "col"), None),
        check_vma=False,
    )
```

```python
import math

import jax
import jax.numpy as jnp
from jax import lax
from jax.experimental import pallas as pl
from jax.experimental.pallas import tpu as pltpu
from jax.sharding import PartitionSpec as P


ROOT_LOG2E = math.sqrt(math.log2(math.e))
NT = (((1,), (1,)), ((), ()))
LANES = 128
HALF = 64
AXES = ("row", "col")
VMEM = pl.BlockSpec(memory_space=pltpu.VMEM)


def place(x, y, z, core):
    return ((y % 2) * 8 + x * 2 + core) * 8 + (y // 2) * 4 + z


def swap(value, *steps):
    pairs = []
    for x in range(4):
        for y in range(4):
            for z in range(4):
                for core in range(2):
                    to = {"x": x, "y": y, "z": z}
                    for step in steps:
                        axis, flip = step[core]
                        to[axis] ^= flip
                    pairs.append((place(x, y, z, core), place(to["x"], to["y"], to["z"], core)))
    return lax.ppermute(value, AXES, pairs)


def partner(value):
    return lax.ppermute(value, AXES, [(i, i ^ 8) for i in range(128)])


def augment(pair, is_col):
    count = pair.shape[0]
    wide = pair.astype(jnp.float32)
    swapped = pltpu.roll(wide, HALF, 1)
    whole = wide + swapped
    norm = jnp.sum(whole * whole, axis=1, keepdims=True) * -0.25
    first = norm.astype(jnp.bfloat16).astype(jnp.float32)
    rest = norm - first
    second = rest.astype(jnp.bfloat16).astype(jnp.float32)
    third = rest - second
    lane = lax.broadcasted_iota(jnp.int32, (count, LANES), 1)
    at, ones = (HALF + 3, HALF) if is_col else (HALF, HALF + 3)
    extra = jnp.where((lane >= ones) & (lane < ones + 3), 1.0, 0.0)
    extra = jnp.where(lane == at, first, extra)
    extra = jnp.where(lane == at + 1, second, extra)
    extra = jnp.where(lane == at + 2, third, extra)
    low = lane < HALF
    if is_col:
        return pair, jnp.where(low, wide, extra).astype(jnp.bfloat16)
    return jnp.where(low, wide, swapped).astype(jnp.bfloat16), jnp.where(low, swapped, extra).astype(jnp.bfloat16)


def pack_own(embeddings_t, inv_length, probes):
    block, width = probes.shape

    def body(emb_hbm, inv_hbm, probe_hbm, own_ref, pair_ref, emb_ref, inv_ref, sems):
        copies = [
            pltpu.make_async_copy(emb_hbm, emb_ref, sems.at[0]),
            pltpu.make_async_copy(inv_hbm, inv_ref, sems.at[1]),
            pltpu.make_async_copy(probe_hbm, own_ref.at[:, LANES:], sems.at[2]),
        ]
        for copy in copies:
            copy.start()
        copies[0].wait()
        copies[1].wait()
        emb = emb_ref[...]
        twice = jnp.concatenate([emb, emb], axis=0).T
        inv = inv_ref[...]
        scaled = (twice * jnp.concatenate([inv, inv], axis=1)) * ROOT_LOG2E
        high = scaled.astype(jnp.bfloat16).astype(jnp.float32)
        lane = lax.broadcasted_iota(jnp.int32, (block, LANES), 1)
        pair = jnp.where(lane < HALF, high, scaled - high).astype(jnp.bfloat16)
        pair_ref[...] = pair
        own_ref[:, :LANES] = pair
        copies[2].wait()

    return pl.pallas_call(
        body,
        in_specs=[pl.BlockSpec(memory_space=pltpu.HBM)] * 3,
        out_specs=[VMEM] * 2,
        out_shape=[
            jax.ShapeDtypeStruct((block, LANES + width), jnp.bfloat16),
            jax.ShapeDtypeStruct((block, LANES), jnp.bfloat16),
        ],
        scratch_shapes=[
            pltpu.VMEM(embeddings_t.shape, jnp.float32),
            pltpu.VMEM(inv_length.shape, jnp.float32),
            pltpu.SemaphoreType.DMA((3,)),
        ],
        compiler_params=pltpu.CompilerParams(vmem_limit_bytes=64900 << 10),
        name="pack_own",
    )(embeddings_t, inv_length, probes)


def join(a, b):
    width = b.shape[1]

    def body(a_ref, b_ref, out_ref):
        out_ref[: a.shape[0], :] = a_ref[:, :width]
        out_ref[a.shape[0] :, :] = b_ref[...]

    return pl.pallas_call(
        body,
        in_specs=[VMEM] * 2,
        out_specs=VMEM,
        out_shape=jax.ShapeDtypeStruct((a.shape[0] + b.shape[0], width), a.dtype),
        compiler_params=pltpu.CompilerParams(vmem_limit_bytes=8 << 20),
    )(a, b)


def prepare_rows(block, sources, groups):
    def body(*refs):
        ins, outs = refs[: len(sources)], refs[len(sources) :]
        for group, out in zip(groups, outs, strict=True):
            for i, (source, k) in enumerate(group):
                a, b = augment(ins[source][k * block : (k + 1) * block, :], False)
                out[i * block : (i + 1) * block, :LANES] = a
                out[i * block : (i + 1) * block, LANES:] = b

    return pl.pallas_call(
        body,
        in_specs=[VMEM] * len(sources),
        out_specs=[VMEM] * len(groups),
        out_shape=[jax.ShapeDtypeStruct((len(g) * block, 2 * LANES), jnp.bfloat16) for g in groups],
        compiler_params=pltpu.CompilerParams(vmem_limit_bytes=12 << 20),
    )(*sources)


def params(mib):
    return pltpu.CompilerParams(vmem_limit_bytes=mib << 20)


def cost(rows, cols, width):
    return pl.CostEstimate(
        flops=4 * rows * cols * 2 * LANES, transcendentals=rows * cols, bytes_accessed=4 * rows * width
    )


def fold(row_ref, at, column, probe):
    gram = lax.dot_general(row_ref[at, :], column, NT, preferred_element_type=jnp.float32)
    return jnp.dot(jnp.exp2(gram).astype(jnp.bfloat16), probe, preferred_element_type=jnp.float32)


def accumulate(rows, olds, packs, out_types):
    n, m, p = len(rows), len(olds), len(packs)
    width = packs[0].shape[1] - LANES
    cols = sum(q.shape[0] for q in packs)
    block = 384

    def body(*refs):
        row_refs, old_refs, pack_refs = refs[:n], refs[n : n + m], refs[n + m : n + m + p]
        out_refs, (right, probes) = refs[n + m + p : -2], refs[-2:]
        start = 0
        for src in pack_refs:
            for k in range(0, src.shape[0], block):
                a, b = augment(src[k : k + block, :LANES], True)
                right[start : start + block, :LANES] = a
                right[start : start + block, LANES:] = b
                probes[start : start + block, :] = src[k : k + block, LANES:]
                start += block
        for k in range(n):
            part = fold(row_refs[k], slice(None), right[...], probes[...])
            out_refs[k][...] = (old_refs[k][...] + part if m else part).astype(out_refs[k].dtype)

    return pl.pallas_call(
        body,
        in_specs=[VMEM] * (n + m + p),
        out_specs=[VMEM] * (n + 2),
        out_shape=[jax.ShapeDtypeStruct((r.shape[0], width), t) for r, t in zip(rows, out_types, strict=True)]
        + [jax.ShapeDtypeStruct((cols, 2 * LANES), jnp.bfloat16), jax.ShapeDtypeStruct((cols, width), jnp.bfloat16)],
        cost_estimate=cost(sum(r.shape[0] for r in rows), cols, width),
        compiler_params=params(28),
    )(*rows, *olds, *packs)


def apply_rows(rows, old, columns, out_type):
    count, width = rows.shape[0], columns[0][1].shape[1]
    flat = [a for pair in columns for a in pair]
    lead = [rows] if old is None else [rows, old]

    def body(*refs):
        row_ref, out_ref, rest = refs[0], refs[-1], refs[len(lead) : -1]
        part = None if old is None else refs[1][...]
        for k in range(0, len(rest), 2):
            more = fold(row_ref, slice(None), rest[k][...], rest[k + 1][...])
            part = more if part is None else part + more
        out_ref[...] = part.astype(out_type)

    return pl.pallas_call(
        body,
        in_specs=[VMEM] * (len(lead) + len(flat)),
        out_specs=VMEM,
        out_shape=jax.ShapeDtypeStruct((count, width), out_type),
        cost_estimate=cost(count, sum(c[0].shape[0] for c in columns), width),
        compiler_params=params(28),
    )(*lead, *flat)


COL_MOVES = ((("x", 1), ("x", 3)), (("x", 3), ("y", 1)), (("y", 1), ("x", 1)))
ROW_MOVES = ((("z", 1), ("z", 3)), (("z", 3), ("y", 3)), (("y", 3), ("z", 1)))


def diagonal(noise, probes):
    return lax.optimization_barrier(noise[:, None] * probes.astype(jnp.float32))


def on_device(embeddings, inv_length, noise, probes):
    block = probes.shape[0]
    f32, bf16 = jnp.float32, jnp.bfloat16
    move_a, move_b, move_c = COL_MOVES
    move_p, move_q, move_r = ROW_MOVES
    own, pair = pack_own(embeddings.T, inv_length[None, :], probes)
    diag = diagonal(noise, probes)

    got_a = swap(own, move_a)
    rows_p = swap(pair, move_p)
    pairs = join(own, rows_p)
    rows_q = swap(pairs, move_q)
    pack_a = join(own, got_a)
    pack_b = swap(pack_a, move_b)
    pack_c = swap(pack_a, move_c)
    other_a = partner(pack_a)
    quads = join(pairs, rows_q)
    rows_r = swap(quads, move_r)

    near = prepare_rows(block, [quads], [[(0, 2), (0, 3)], [(0, 1)], [(0, 0)]])
    row_n, row_p, row_own = near
    n, beside, total, *aug_a = accumulate(near, [], [pack_a, other_a], [f32, f32, f32])

    other_b, other_c = partner(pack_b), partner(pack_c)
    pack_d = swap(pack_b, move_c)
    far = prepare_rows(block, [rows_r], [[(0, 2), (0, 3)], [(0, 0), (0, 1)]])
    row_f1, row_f2 = far
    f1 = apply_rows(row_f1, None, [aug_a], f32)
    f1, *aug_b = accumulate([row_f1], [f1], [pack_b, other_b], [f32])
    f1, *aug_c = accumulate([row_f1], [f1], [pack_c, other_c], [f32])
    f2 = apply_rows(row_f2, None, [aug_a], f32)
    other_d = partner(pack_d)
    f2 = apply_rows(row_f2, f2, [aug_b, aug_c], f32)
    f1, *aug_d = accumulate([row_f1], [f1], [pack_d, other_d], [bf16])
    in_1 = swap(f1, move_r)
    f2 = apply_rows(row_f2, f2, [aug_d], bf16)
    in_2 = swap(f2, move_r)

    columns = [aug_b, aug_c, aug_d]
    n = apply_rows(row_n, n, columns, f32)
    beside = apply_rows(row_p, beside, columns, f32)
    from_q = swap((n[:block] + in_1[:block].astype(f32)).astype(bf16), move_q)
    from_qp = swap((n[block:] + in_1[block:].astype(f32)).astype(bf16), move_q, move_p)
    from_p = swap((beside + in_2[block:].astype(f32)).astype(bf16), move_p)
    total = apply_rows(row_own, total, columns, f32)
    total = total + diag + in_2[:block].astype(f32)
    return total + from_q.astype(f32) + from_qp.astype(f32) + from_p.astype(f32)


def solution(mesh):
    return jax.shard_map(
        on_device,
        mesh=mesh,
        in_specs=(P(("row", "col"), None), P(), P(("row", "col")), P(("row", "col"), None)),
        out_specs=P(("row", "col"), None),
        check_vma=False,
    )
```

```python
import math

import jax
import jax.numpy as jnp
from jax import lax
from jax.experimental import pallas as pl
from jax.experimental.pallas import tpu as pltpu
from jax.sharding import PartitionSpec as P


ROOT_LOG2E = math.sqrt(math.log2(math.e))
NT = (((1,), (1,)), ((), ()))
LANES = 128
HALF = 64
AXES = ("row", "col")
VMEM = pl.BlockSpec(memory_space=pltpu.VMEM)


def place(x, y, z, core):
    return ((y % 2) * 8 + x * 2 + core) * 8 + (y // 2) * 4 + z


def swap(value, *steps):
    pairs = []
    for x in range(4):
        for y in range(4):
            for z in range(4):
                for core in range(2):
                    to = {"x": x, "y": y, "z": z}
                    for step in steps:
                        axis, flip = step[core]
                        to[axis] ^= flip
                    pairs.append((place(x, y, z, core), place(to["x"], to["y"], to["z"], core)))
    return lax.ppermute(value, AXES, pairs)


def partner(value):
    return lax.ppermute(value, AXES, [(i, i ^ 8) for i in range(128)])


def augment(pair, is_col):
    count = pair.shape[0]
    wide = pair.astype(jnp.float32)
    swapped = pltpu.roll(wide, HALF, 1)
    whole = wide + swapped
    norm = jnp.sum(whole * whole, axis=1, keepdims=True) * -0.25
    first = norm.astype(jnp.bfloat16).astype(jnp.float32)
    rest = norm - first
    second = rest.astype(jnp.bfloat16).astype(jnp.float32)
    third = rest - second
    lane = lax.broadcasted_iota(jnp.int32, (count, LANES), 1)
    at, ones = (HALF + 3, HALF) if is_col else (HALF, HALF + 3)
    extra = jnp.where((lane >= ones) & (lane < ones + 3), 1.0, 0.0)
    extra = jnp.where(lane == at, first, extra)
    extra = jnp.where(lane == at + 1, second, extra)
    extra = jnp.where(lane == at + 2, third, extra)
    low = lane < HALF
    if is_col:
        return pair, jnp.where(low, wide, extra).astype(jnp.bfloat16)
    return jnp.where(low, wide, swapped).astype(jnp.bfloat16), jnp.where(low, swapped, extra).astype(jnp.bfloat16)


def pack_own(embeddings_t, inv_length, probes):
    block, width = probes.shape

    def body(emb_hbm, inv_hbm, probe_hbm, own_ref, pair_ref, emb_ref, inv_ref, sems):
        copies = [
            pltpu.make_async_copy(emb_hbm, emb_ref, sems.at[0]),
            pltpu.make_async_copy(inv_hbm, inv_ref, sems.at[1]),
            pltpu.make_async_copy(probe_hbm, own_ref.at[:, LANES:], sems.at[2]),
        ]
        for copy in copies:
            copy.start()
        copies[0].wait()
        copies[1].wait()
        emb = emb_ref[...]
        twice = jnp.concatenate([emb, emb], axis=0).T
        inv = inv_ref[...]
        scaled = (twice * jnp.concatenate([inv, inv], axis=1)) * ROOT_LOG2E
        high = scaled.astype(jnp.bfloat16).astype(jnp.float32)
        lane = lax.broadcasted_iota(jnp.int32, (block, LANES), 1)
        pair = jnp.where(lane < HALF, high, scaled - high).astype(jnp.bfloat16)
        pair_ref[...] = pair
        own_ref[:, :LANES] = pair
        copies[2].wait()

    return pl.pallas_call(
        body,
        in_specs=[pl.BlockSpec(memory_space=pltpu.HBM)] * 3,
        out_specs=[VMEM] * 2,
        out_shape=[
            jax.ShapeDtypeStruct((block, LANES + width), jnp.bfloat16),
            jax.ShapeDtypeStruct((block, LANES), jnp.bfloat16),
        ],
        scratch_shapes=[
            pltpu.VMEM(embeddings_t.shape, jnp.float32),
            pltpu.VMEM(inv_length.shape, jnp.float32),
            pltpu.SemaphoreType.DMA((3,)),
        ],
        compiler_params=pltpu.CompilerParams(vmem_limit_bytes=64900 << 10),
        name="pack_own",
    )(embeddings_t, inv_length, probes)


def join(first, *others):
    count, width = others[0].shape

    def body(*refs):
        out_ref = refs[-1]
        out_ref[:count, :] = refs[0][:, :width]
        for i, ref in enumerate(refs[1:-1], 1):
            out_ref[i * count : (i + 1) * count, :] = ref[...]

    return pl.pallas_call(
        body,
        in_specs=[VMEM] * (1 + len(others)),
        out_specs=VMEM,
        out_shape=jax.ShapeDtypeStruct(((1 + len(others)) * count, width), first.dtype),
        compiler_params=pltpu.CompilerParams(vmem_limit_bytes=8 << 20),
    )(first, *others)


def prepare_rows(block, sources, groups):
    def body(*refs):
        ins, outs = refs[: len(sources)], refs[len(sources) :]
        for group, out in zip(groups, outs, strict=True):
            for i, (source, k) in enumerate(group):
                a, b = augment(ins[source][k * block : (k + 1) * block, :], False)
                out[i * block : (i + 1) * block, :LANES] = a
                out[i * block : (i + 1) * block, LANES:] = b

    return pl.pallas_call(
        body,
        in_specs=[VMEM] * len(sources),
        out_specs=[VMEM] * len(groups),
        out_shape=[jax.ShapeDtypeStruct((len(g) * block, 2 * LANES), jnp.bfloat16) for g in groups],
        compiler_params=pltpu.CompilerParams(vmem_limit_bytes=12 << 20),
    )(*sources)


def params(mib):
    return pltpu.CompilerParams(vmem_limit_bytes=mib << 20)


def cost(rows, cols, width):
    return pl.CostEstimate(
        flops=4 * rows * cols * 2 * LANES, transcendentals=rows * cols, bytes_accessed=4 * rows * width
    )


def fold(row_ref, at, column, probe):
    gram = lax.dot_general(row_ref[at, :], column, NT, preferred_element_type=jnp.float32)
    return jnp.dot(jnp.exp2(gram).astype(jnp.bfloat16), probe, preferred_element_type=jnp.float32)


def accumulate(rows, olds, packs, out_types):
    n, m, p = len(rows), len(olds), len(packs)
    width = packs[0].shape[1] - LANES
    cols = sum(q.shape[0] for q in packs)
    block = 384

    def body(*refs):
        row_refs, old_refs, pack_refs = refs[:n], refs[n : n + m], refs[n + m : n + m + p]
        out_refs, (right, probes) = refs[n + m + p : -2], refs[-2:]
        start = 0
        for src in pack_refs:
            for k in range(0, src.shape[0], block):
                a, b = augment(src[k : k + block, :LANES], True)
                right[start : start + block, :LANES] = a
                right[start : start + block, LANES:] = b
                probes[start : start + block, :] = src[k : k + block, LANES:]
                start += block
        for k in range(n):
            part = fold(row_refs[k], slice(None), right[...], probes[...])
            out_refs[k][...] = (old_refs[k][...] + part if m else part).astype(out_refs[k].dtype)

    return pl.pallas_call(
        body,
        in_specs=[VMEM] * (n + m + p),
        out_specs=[VMEM] * (n + 2),
        out_shape=[jax.ShapeDtypeStruct((r.shape[0], width), t) for r, t in zip(rows, out_types, strict=True)]
        + [jax.ShapeDtypeStruct((cols, 2 * LANES), jnp.bfloat16), jax.ShapeDtypeStruct((cols, width), jnp.bfloat16)],
        cost_estimate=cost(sum(r.shape[0] for r in rows), cols, width),
        compiler_params=params(28),
    )(*rows, *olds, *packs)


def apply_rows(rows, old, columns, out_type):
    count, width = rows.shape[0], columns[0][1].shape[1]
    flat = [a for pair in columns for a in pair]
    lead = [rows] if old is None else [rows, old]

    def body(*refs):
        row_ref, out_ref, rest = refs[0], refs[-1], refs[len(lead) : -1]
        part = None if old is None else refs[1][...]
        for k in range(0, len(rest), 2):
            more = fold(row_ref, slice(None), rest[k][...], rest[k + 1][...])
            part = more if part is None else part + more
        out_ref[...] = part.astype(out_type)

    return pl.pallas_call(
        body,
        in_specs=[VMEM] * (len(lead) + len(flat)),
        out_specs=VMEM,
        out_shape=jax.ShapeDtypeStruct((count, width), out_type),
        cost_estimate=cost(count, sum(c[0].shape[0] for c in columns), width),
        compiler_params=params(28),
    )(*lead, *flat)


def apply_each(rows, columns):
    n, width = len(rows), columns[0][1].shape[1]
    flat = [a for pair in columns for a in pair]

    def body(*refs):
        rest, outs = refs[n : n + len(flat)], refs[n + len(flat) :]
        for row_ref, out_ref in zip(refs[:n], outs, strict=True):
            out_ref[...] = sum(
                fold(row_ref, slice(None), rest[k][...], rest[k + 1][...]) for k in range(0, len(rest), 2)
            )

    return pl.pallas_call(
        body,
        in_specs=[VMEM] * (n + len(flat)),
        out_specs=[VMEM] * n,
        out_shape=[jax.ShapeDtypeStruct((r.shape[0], width), jnp.float32) for r in rows],
        cost_estimate=cost(sum(r.shape[0] for r in rows), sum(c[0].shape[0] for c in columns), width),
        compiler_params=params(28),
    )(*rows, *flat)


COL_MOVES = ((("x", 1), ("x", 3)), (("x", 3), ("y", 1)), (("y", 1), ("x", 1)))
ROW_MOVES = ((("z", 1), ("z", 3)), (("z", 3), ("y", 3)), (("y", 3), ("z", 1)))


def diagonal(noise, probes):
    return lax.optimization_barrier(noise[:, None] * probes.astype(jnp.float32))


def on_device(embeddings, inv_length, noise, probes):
    block = probes.shape[0]
    f32, bf16 = jnp.float32, jnp.bfloat16
    move_a, move_b, move_c = COL_MOVES
    move_p, move_q, move_r = ROW_MOVES
    own, pair = pack_own(embeddings.T, inv_length[None, :], probes)
    diag = diagonal(noise, probes)

    got_a = swap(own, move_a)
    rows_p = swap(pair, move_p)
    rows_q = swap(pair, move_q)
    rows_qp = swap(pair, move_q, move_p)
    pack_a = join(own, got_a)
    pack_b = swap(pack_a, move_b)
    quads = join(own, rows_p, rows_q, rows_qp)
    rows_r = swap(quads, move_r)
    other_a = partner(pack_a)
    pack_c = swap(pack_a, move_c)

    near = prepare_rows(block, [quads], [[(0, 2), (0, 3)], [(0, 1)], [(0, 0)]])
    row_n, row_p, row_own = near
    n, beside, total, *aug_a = accumulate(near, [], [pack_a, other_a], [f32, f32, f32])

    other_b, other_c = partner(pack_b), partner(pack_c)
    pack_d = swap(pack_b, move_c)
    far = prepare_rows(block, [rows_r], [[(0, 2), (0, 3)], [(0, 0), (0, 1)]])
    row_f1, row_f2 = far
    f1, f2 = apply_each(far, [aug_a])
    f1, *aug_b = accumulate([row_f1], [f1], [pack_b, other_b], [f32])
    f1, *aug_c = accumulate([row_f1], [f1], [pack_c, other_c], [f32])
    other_d = partner(pack_d)
    f2 = apply_rows(row_f2, f2, [aug_b, aug_c], f32)
    f1, *aug_d = accumulate([row_f1], [f1], [pack_d, other_d], [bf16])
    in_1 = swap(f1, move_r)
    f2 = apply_rows(row_f2, f2, [aug_d], bf16)
    in_2 = swap(f2, move_r)

    columns = [aug_b, aug_c, aug_d]
    n = apply_rows(row_n, n, columns, f32)
    from_q = swap((n[:block] + in_1[:block].astype(f32)).astype(bf16), move_q)
    from_qp = swap((n[block:] + in_1[block:].astype(f32)).astype(bf16), move_q, move_p)
    beside = apply_rows(row_p, beside, columns, f32)
    from_p = swap((beside + in_2[block:].astype(f32)).astype(bf16), move_p)
    total = apply_rows(row_own, total, columns, f32)
    total = total + diag + in_2[:block].astype(f32)
    return total + from_q.astype(f32) + from_qp.astype(f32) + from_p.astype(f32)


def solution(mesh):
    return jax.shard_map(
        on_device,
        mesh=mesh,
        in_specs=(P(("row", "col"), None), P(), P(("row", "col")), P(("row", "col"), None)),
        out_specs=P(("row", "col"), None),
        check_vma=False,
    )
```

```python
import math

import jax
import jax.numpy as jnp
from jax import lax
from jax.experimental import pallas as pl
from jax.experimental.pallas import tpu as pltpu
from jax.sharding import PartitionSpec as P


ROOT_LOG2E = math.sqrt(math.log2(math.e))
NT = (((1,), (1,)), ((), ()))
LANES = 128
HALF = 64
BLOCK = 384
AXES = ("row", "col")
VMEM = pl.BlockSpec(memory_space=pltpu.VMEM)


def place(x, y, z, core):
    return ((y % 2) * 8 + x * 2 + core) * 8 + (y // 2) * 4 + z


def swap(value, *steps):
    pairs = []
    for x in range(4):
        for y in range(4):
            for z in range(4):
                for core in range(2):
                    to = {"x": x, "y": y, "z": z}
                    for step in steps:
                        axis, flip = step[core]
                        to[axis] ^= flip
                    pairs.append((place(x, y, z, core), place(to["x"], to["y"], to["z"], core)))
    return lax.ppermute(value, AXES, pairs)


def partner(value):
    return lax.ppermute(value, AXES, [(i, i ^ 8) for i in range(128)])


def augment(pair, is_col):
    count = pair.shape[0]
    wide = pair.astype(jnp.float32)
    swapped = pltpu.roll(wide, HALF, 1)
    whole = wide + swapped
    norm = jnp.sum(whole * whole, axis=1, keepdims=True) * -0.25
    first = norm.astype(jnp.bfloat16).astype(jnp.float32)
    rest = norm - first
    second = rest.astype(jnp.bfloat16).astype(jnp.float32)
    third = rest - second
    lane = lax.broadcasted_iota(jnp.int32, (count, LANES), 1)
    at, ones = (HALF + 3, HALF) if is_col else (HALF, HALF + 3)
    extra = jnp.where((lane >= ones) & (lane < ones + 3), 1.0, 0.0)
    extra = jnp.where(lane == at, first, extra)
    extra = jnp.where(lane == at + 1, second, extra)
    extra = jnp.where(lane == at + 2, third, extra)
    low = lane < HALF
    if is_col:
        return pair, jnp.where(low, wide, extra).astype(jnp.bfloat16)
    return jnp.where(low, wide, swapped).astype(jnp.bfloat16), jnp.where(low, swapped, extra).astype(jnp.bfloat16)


def pack_own(embeddings_t, inv_length, probes):
    block, width = probes.shape

    def body(emb_hbm, inv_hbm, probe_hbm, own_ref, pair_ref, emb_ref, inv_ref, sems):
        copies = [
            pltpu.make_async_copy(emb_hbm, emb_ref, sems.at[0]),
            pltpu.make_async_copy(inv_hbm, inv_ref, sems.at[1]),
            pltpu.make_async_copy(probe_hbm, own_ref.at[:, LANES:], sems.at[2]),
        ]
        for copy in copies:
            copy.start()
        copies[0].wait()
        copies[1].wait()
        emb = emb_ref[...]
        twice = jnp.concatenate([emb, emb], axis=0).T
        inv = inv_ref[...]
        scaled = (twice * jnp.concatenate([inv, inv], axis=1)) * ROOT_LOG2E
        high = scaled.astype(jnp.bfloat16).astype(jnp.float32)
        lane = lax.broadcasted_iota(jnp.int32, (block, LANES), 1)
        pair = jnp.where(lane < HALF, high, scaled - high).astype(jnp.bfloat16)
        pair_ref[...] = pair
        own_ref[:, :LANES] = pair
        copies[2].wait()

    return pl.pallas_call(
        body,
        in_specs=[pl.BlockSpec(memory_space=pltpu.HBM)] * 3,
        out_specs=[VMEM] * 2,
        out_shape=[
            jax.ShapeDtypeStruct((block, LANES + width), jnp.bfloat16),
            jax.ShapeDtypeStruct((block, LANES), jnp.bfloat16),
        ],
        scratch_shapes=[
            pltpu.VMEM(embeddings_t.shape, jnp.float32),
            pltpu.VMEM(inv_length.shape, jnp.float32),
            pltpu.SemaphoreType.DMA((3,)),
        ],
        compiler_params=pltpu.CompilerParams(vmem_limit_bytes=64900 << 10),
        name="pack_own",
    )(embeddings_t, inv_length, probes)


def join(first, *others):
    count, width = others[0].shape

    def body(*refs):
        out_ref = refs[-1]
        out_ref[:count, :] = refs[0][:, :width]
        for i, ref in enumerate(refs[1:-1], 1):
            out_ref[i * count : (i + 1) * count, :] = ref[...]

    return pl.pallas_call(
        body,
        in_specs=[VMEM] * (1 + len(others)),
        out_specs=VMEM,
        out_shape=jax.ShapeDtypeStruct(((1 + len(others)) * count, width), first.dtype),
        compiler_params=pltpu.CompilerParams(vmem_limit_bytes=8 << 20),
    )(first, *others)


def params(mib):
    return pltpu.CompilerParams(vmem_limit_bytes=mib << 20)


def cost(rows, cols, width):
    return pl.CostEstimate(
        flops=4 * rows * cols * 2 * LANES, transcendentals=rows * cols, bytes_accessed=4 * rows * width
    )


def fold(row_ref, at, column, probe):
    gram = lax.dot_general(row_ref[at, :], column, NT, preferred_element_type=jnp.float32)
    return jnp.dot(jnp.exp2(gram).astype(jnp.bfloat16), probe, preferred_element_type=jnp.float32)


def fill_rows(pair_ref, left):
    for k in range(0, pair_ref.shape[0], BLOCK):
        a, b = augment(pair_ref[k : k + BLOCK, :], False)
        left[k : k + BLOCK, :LANES] = a
        left[k : k + BLOCK, LANES:] = b


def fill_columns(pack_refs, right, probes):
    start = 0
    for src in pack_refs:
        for k in range(0, src.shape[0], BLOCK):
            a, b = augment(src[k : k + BLOCK, :LANES], True)
            right[start : start + BLOCK, :LANES] = a
            right[start : start + BLOCK, LANES:] = b
            probes[start : start + BLOCK, :] = src[k : k + BLOCK, LANES:]
            start += BLOCK


def columns_shape(packs):
    cols = sum(q.shape[0] for q in packs)
    width = packs[0].shape[1] - LANES
    return [jax.ShapeDtypeStruct((cols, 2 * LANES), jnp.bfloat16), jax.ShapeDtypeStruct((cols, width), jnp.bfloat16)]


def first_round(pairs, cuts, packs, columns):
    count = pairs.shape[0]
    shape = columns_shape(packs) if packs else [columns[0], columns[1]]
    width, cols = shape[1].shape[1], shape[1].shape[0]
    sides = packs or list(columns)

    def body(*refs):
        pair_ref, side_refs, outs = refs[0], refs[1 : 1 + len(sides)], refs[1 + len(sides) :]
        left, sums = outs[0], outs[1 : len(cuts) + 1]
        right, probes = outs[-2:] if packs else side_refs
        fill_rows(pair_ref, left)
        if packs:
            fill_columns(side_refs, right, probes)
        part = fold(left, slice(None), right[...], probes[...])
        for at, ref in zip(cuts, sums, strict=True):
            ref[...] = part[at : at + ref.shape[0], :]

    ends = cuts[1:] + [count]
    return pl.pallas_call(
        body,
        in_specs=[VMEM] * (1 + len(sides)),
        out_specs=[VMEM] * (1 + len(cuts) + (2 if packs else 0)),
        out_shape=[jax.ShapeDtypeStruct((count, 2 * LANES), jnp.bfloat16)]
        + [jax.ShapeDtypeStruct((end - at, width), jnp.float32) for at, end in zip(cuts, ends, strict=True)]
        + (shape if packs else []),
        cost_estimate=cost(count, cols, width),
        compiler_params=params(36),
    )(pairs, *sides)


def accumulate(rows, at, old, packs, out_type):
    count, width = old.shape
    shape = columns_shape(packs)

    def body(*refs):
        row_ref, old_ref, pack_refs, (out_ref, right, probes) = refs[0], refs[1], refs[2:-3], refs[-3:]
        fill_columns(pack_refs, right, probes)
        part = fold(row_ref, pl.ds(at, count), right[...], probes[...])
        out_ref[...] = (old_ref[...] + part).astype(out_type)

    return pl.pallas_call(
        body,
        in_specs=[VMEM] * (2 + len(packs)),
        out_specs=[VMEM] * 3,
        out_shape=[jax.ShapeDtypeStruct((count, width), out_type)] + shape,
        cost_estimate=cost(count, shape[0].shape[0], width),
        compiler_params=params(28),
    )(rows, old, *packs)


def apply_rows(rows, at, old, columns, out_type):
    count, width = old.shape
    flat = [a for pair in columns for a in pair]

    def body(*refs):
        row_ref, old_ref, rest, out_ref = refs[0], refs[1], refs[2:-1], refs[-1]
        part = old_ref[...]
        for k in range(0, len(rest), 2):
            part = part + fold(row_ref, pl.ds(at, count), rest[k][...], rest[k + 1][...])
        out_ref[...] = part.astype(out_type)

    return pl.pallas_call(
        body,
        in_specs=[VMEM] * (2 + len(flat)),
        out_specs=VMEM,
        out_shape=jax.ShapeDtypeStruct((count, width), out_type),
        cost_estimate=cost(count, sum(c[0].shape[0] for c in columns), width),
        compiler_params=params(28),
    )(rows, old, *flat)


COL_MOVES = ((("x", 1), ("x", 3)), (("x", 3), ("y", 1)), (("y", 1), ("x", 1)))
ROW_MOVES = ((("z", 1), ("z", 3)), (("z", 3), ("y", 3)), (("y", 3), ("z", 1)))


def diagonal(noise, probes):
    return lax.optimization_barrier(noise[:, None] * probes.astype(jnp.float32))


def on_device(embeddings, inv_length, noise, probes):
    block = probes.shape[0]
    f32, bf16 = jnp.float32, jnp.bfloat16
    move_a, move_b, move_c = COL_MOVES
    move_p, move_q, move_r = ROW_MOVES
    own, pair = pack_own(embeddings.T, inv_length[None, :], probes)
    diag = diagonal(noise, probes)

    got_a = swap(own, move_a)
    rows_p = swap(pair, move_p)
    rows_q = swap(pair, move_q)
    rows_qp = swap(pair, move_q, move_p)
    pack_a = join(own, got_a)
    pack_b = swap(pack_a, move_b)
    quads = join(own, rows_p, rows_q, rows_qp)
    rows_r = swap(quads, move_r)
    other_a = partner(pack_a)
    pack_c = swap(pack_a, move_c)

    near, total, beside, n, *aug_a = first_round(quads, [0, block, 2 * block], [pack_a, other_a], None)

    other_b, other_c = partner(pack_b), partner(pack_c)
    pack_d = swap(pack_b, move_c)
    far, f2, f1 = first_round(rows_r, [0, 2 * block], [], aug_a)
    f1, *aug_b = accumulate(far, 2 * block, f1, [pack_b, other_b], f32)
    f1, *aug_c = accumulate(far, 2 * block, f1, [pack_c, other_c], f32)
    other_d = partner(pack_d)
    f2 = apply_rows(far, 0, f2, [aug_b, aug_c], f32)
    f1, *aug_d = accumulate(far, 2 * block, f1, [pack_d, other_d], bf16)
    in_1 = swap(f1, move_r)
    f2 = apply_rows(far, 0, f2, [aug_d], bf16)
    in_2 = swap(f2, move_r)

    columns = [aug_b, aug_c, aug_d]
    n = apply_rows(near, 2 * block, n, columns, f32)
    from_q = swap((n[:block] + in_1[:block].astype(f32)).astype(bf16), move_q)
    from_qp = swap((n[block:] + in_1[block:].astype(f32)).astype(bf16), move_q, move_p)
    beside = apply_rows(near, block, beside, columns, f32)
    from_p = swap((beside + in_2[block:].astype(f32)).astype(bf16), move_p)
    total = apply_rows(near, 0, total, columns, f32)
    total = total + diag + in_2[:block].astype(f32)
    return total + from_q.astype(f32) + from_qp.astype(f32) + from_p.astype(f32)


def solution(mesh):
    return jax.shard_map(
        on_device,
        mesh=mesh,
        in_specs=(P(("row", "col"), None), P(), P(("row", "col")), P(("row", "col"), None)),
        out_specs=P(("row", "col"), None),
        check_vma=False,
    )
```

```python
import math

import jax
import jax.numpy as jnp
from jax import lax
from jax.experimental import pallas as pl
from jax.experimental.pallas import tpu as pltpu
from jax.sharding import PartitionSpec as P


ROOT_LOG2E = math.sqrt(math.log2(math.e))
NT = (((1,), (1,)), ((), ()))
LANES = 128
HALF = 64
BLOCK = 384
AXES = ("row", "col")
VMEM = pl.BlockSpec(memory_space=pltpu.VMEM)


def place(x, y, z, core):
    return ((y % 2) * 8 + x * 2 + core) * 8 + (y // 2) * 4 + z


def swap(value, *steps):
    pairs = []
    for x in range(4):
        for y in range(4):
            for z in range(4):
                for core in range(2):
                    to = {"x": x, "y": y, "z": z}
                    for step in steps:
                        axis, flip = step[core]
                        to[axis] ^= flip
                    pairs.append((place(x, y, z, core), place(to["x"], to["y"], to["z"], core)))
    return lax.ppermute(value, AXES, pairs)


def partner(value):
    return lax.ppermute(value, AXES, [(i, i ^ 8) for i in range(128)])


def augment(pair, is_col):
    count = pair.shape[0]
    wide = pair.astype(jnp.float32)
    swapped = pltpu.roll(wide, HALF, 1)
    whole = wide + swapped
    norm = jnp.sum(whole * whole, axis=1, keepdims=True) * -0.25
    first = norm.astype(jnp.bfloat16).astype(jnp.float32)
    rest = norm - first
    second = rest.astype(jnp.bfloat16).astype(jnp.float32)
    third = rest - second
    lane = lax.broadcasted_iota(jnp.int32, (count, LANES), 1)
    at, ones = (HALF + 3, HALF) if is_col else (HALF, HALF + 3)
    extra = jnp.where((lane >= ones) & (lane < ones + 3), 1.0, 0.0)
    extra = jnp.where(lane == at, first, extra)
    extra = jnp.where(lane == at + 1, second, extra)
    extra = jnp.where(lane == at + 2, third, extra)
    low = lane < HALF
    if is_col:
        return pair, jnp.where(low, wide, extra).astype(jnp.bfloat16)
    return jnp.where(low, wide, swapped).astype(jnp.bfloat16), jnp.where(low, swapped, extra).astype(jnp.bfloat16)


def pack_own(embeddings_t, inv_length, probes):
    block, width = probes.shape

    def body(emb_hbm, inv_hbm, probe_hbm, own_ref, pair_ref, emb_ref, inv_ref, sems):
        copies = [
            pltpu.make_async_copy(emb_hbm, emb_ref, sems.at[0]),
            pltpu.make_async_copy(inv_hbm, inv_ref, sems.at[1]),
            pltpu.make_async_copy(probe_hbm, own_ref.at[:, LANES:], sems.at[2]),
        ]
        for copy in copies:
            copy.start()
        copies[0].wait()
        copies[1].wait()
        emb = emb_ref[...]
        twice = jnp.concatenate([emb, emb], axis=0).T
        inv = inv_ref[...]
        scaled = (twice * jnp.concatenate([inv, inv], axis=1)) * ROOT_LOG2E
        high = scaled.astype(jnp.bfloat16).astype(jnp.float32)
        lane = lax.broadcasted_iota(jnp.int32, (block, LANES), 1)
        pair = jnp.where(lane < HALF, high, scaled - high).astype(jnp.bfloat16)
        pair_ref[...] = pair
        own_ref[:, :LANES] = pair
        copies[2].wait()

    return pl.pallas_call(
        body,
        in_specs=[pl.BlockSpec(memory_space=pltpu.HBM)] * 3,
        out_specs=[VMEM] * 2,
        out_shape=[
            jax.ShapeDtypeStruct((block, LANES + width), jnp.bfloat16),
            jax.ShapeDtypeStruct((block, LANES), jnp.bfloat16),
        ],
        scratch_shapes=[
            pltpu.VMEM(embeddings_t.shape, jnp.float32),
            pltpu.VMEM(inv_length.shape, jnp.float32),
            pltpu.SemaphoreType.DMA((3,)),
        ],
        compiler_params=pltpu.CompilerParams(vmem_limit_bytes=64900 << 10),
        name="pack_own",
    )(embeddings_t, inv_length, probes)


def join(first, *others):
    count, width = others[0].shape

    def body(*refs):
        out_ref = refs[-1]
        out_ref[:count, :] = refs[0][:, :width]
        for i, ref in enumerate(refs[1:-1], 1):
            out_ref[i * count : (i + 1) * count, :] = ref[...]

    return pl.pallas_call(
        body,
        in_specs=[VMEM] * (1 + len(others)),
        out_specs=VMEM,
        out_shape=jax.ShapeDtypeStruct(((1 + len(others)) * count, width), first.dtype),
        compiler_params=pltpu.CompilerParams(vmem_limit_bytes=8 << 20),
    )(first, *others)


def params(mib):
    return pltpu.CompilerParams(vmem_limit_bytes=mib << 20)


def cost(rows, cols, width):
    return pl.CostEstimate(
        flops=4 * rows * cols * 2 * LANES, transcendentals=rows * cols, bytes_accessed=4 * rows * width
    )


def fold(rows, pack_ref, half):
    column = jnp.concatenate([pack_ref[:, :LANES], half], axis=1)
    gram = lax.dot_general(rows, column, NT, preferred_element_type=jnp.float32)
    return jnp.dot(jnp.exp2(gram).astype(jnp.bfloat16), pack_ref[:, LANES:], preferred_element_type=jnp.float32)


def fill_rows(pair_ref, left):
    for k in range(0, pair_ref.shape[0], BLOCK):
        a, b = augment(pair_ref[k : k + BLOCK, :], False)
        left[k : k + BLOCK, :LANES] = a
        left[k : k + BLOCK, LANES:] = b


def fill_half(pack_ref, half):
    for k in range(0, pack_ref.shape[0], BLOCK):
        half[k : k + BLOCK, :] = augment(pack_ref[k : k + BLOCK, :LANES], True)[1]


def half_of(pack):
    return jax.ShapeDtypeStruct((pack.shape[0], LANES), jnp.bfloat16)


def call(body, inputs, outputs, rows, packs):
    cols = sum(pack.shape[0] for pack in packs)
    return pl.pallas_call(
        body,
        in_specs=[VMEM] * len(inputs),
        out_specs=[VMEM] * len(outputs),
        out_shape=outputs,
        cost_estimate=cost(rows, cols, packs[0].shape[1] - LANES),
        compiler_params=params(28),
    )(*inputs)


def first_round(pairs, cuts, known, packs):
    count, width = pairs.shape[0], (known[0][0] if known else packs[0]).shape[1] - LANES
    ready, fresh, step = len(known), len(packs), 2 * BLOCK
    ends = cuts[1:] + [count]

    def body(*refs):
        pair_ref, refs = refs[0], refs[1:]
        sides = [(refs[2 * i], refs[2 * i + 1]) for i in range(ready)]
        pack_refs, outs = refs[2 * ready : 2 * ready + fresh], refs[2 * ready + fresh :]
        left, sums, halves = outs[0], outs[1 : 1 + len(cuts)], outs[1 + len(cuts) :]
        fill_rows(pair_ref, left)
        for pack_ref, half in zip(pack_refs, halves, strict=True):
            fill_half(pack_ref, half)
            sides.append((pack_ref, half))
        for row in range(0, count, step):
            part = sum(fold(left[row : row + step, :], pack_ref, half[...]) for pack_ref, half in sides)
            for at, end, ref in zip(cuts, ends, sums, strict=True):
                low, high = max(at, row), min(end, row + step)
                if low < high:
                    ref[low - at : high - at, :] = part[low - row : high - row, :]

    return call(
        body,
        [pairs, *(x for side in known for x in side), *packs],
        [jax.ShapeDtypeStruct((count, 2 * LANES), jnp.bfloat16)]
        + [jax.ShapeDtypeStruct((end - at, width), jnp.float32) for at, end in zip(cuts, ends, strict=True)]
        + [half_of(pack) for pack in packs],
        count,
        [side[0] for side in known] + list(packs),
    )


def add_round(rows, at, old, known, packs, out_type):
    count = old.shape[0]
    ready, fresh = len(known), len(packs)

    def body(*refs):
        row_ref, old_ref, refs = refs[0], refs[1], refs[2:]
        sides = [(refs[2 * i], refs[2 * i + 1]) for i in range(ready)]
        pack_refs, out_ref, halves = refs[2 * ready : 2 * ready + fresh], refs[2 * ready + fresh], refs[2 * ready + fresh + 1 :]
        for pack_ref, half in zip(pack_refs, halves, strict=True):
            fill_half(pack_ref, half)
            sides.append((pack_ref, half))
        part = old_ref[...]
        for pack_ref, half in sides:
            part = part + fold(row_ref[at : at + count, :], pack_ref, half[...])
        out_ref[...] = part.astype(out_type)

    return call(
        body,
        [rows, old, *(x for side in known for x in side), *packs],
        [jax.ShapeDtypeStruct(old.shape, out_type)] + [half_of(pack) for pack in packs],
        count,
        [side[0] for side in known] + list(packs),
    )


COL_MOVES = ((("x", 1), ("x", 3)), (("x", 3), ("y", 1)), (("y", 1), ("x", 1)))
ROW_MOVES = ((("z", 1), ("z", 3)), (("z", 3), ("y", 3)), (("y", 3), ("z", 1)))


def diagonal(noise, probes):
    return lax.optimization_barrier(noise[:, None] * probes.astype(jnp.float32))


def on_device(embeddings, inv_length, noise, probes):
    block = probes.shape[0]
    f32, bf16 = jnp.float32, jnp.bfloat16
    move_a, move_b, move_c = COL_MOVES
    move_p, move_q, move_r = ROW_MOVES
    own, pair = pack_own(embeddings.T, inv_length[None, :], probes)
    diag = diagonal(noise, probes)

    got_a, got_b, got_c = (swap(own, m) for m in (move_a, move_b, move_c))
    rows_p = swap(pair, move_p)
    rows_q = swap(pair, move_q)
    rows_qp = swap(pair, move_q, move_p)
    got_ab = swap(got_a, move_b)
    pack_3 = swap(join(got_a, got_b), move_c)
    quads = join(own, rows_p, rows_q, rows_qp)
    rows_r = swap(quads, move_r)
    pack_1 = join(own, got_a)
    other_1 = partner(pack_1)
    pack_2 = join(got_b, got_c)
    other_2 = partner(pack_2)

    near, total, beside, n, *halves = first_round(quads, [0, block, 2 * block], [], [pack_1, other_1])
    side_1 = list(zip([pack_1, other_1], halves, strict=True))

    got_abc = swap(got_ab, move_c)
    other_3 = partner(pack_3)
    far, f2, f1, *halves = first_round(rows_r, [0, 2 * block], side_1, [pack_2, other_2])
    side_2 = list(zip([pack_2, other_2], halves, strict=True))
    pack_4 = join(got_ab, got_abc)
    other_4 = partner(pack_4)
    f1, *halves = add_round(far, 2 * block, f1, [], [pack_3, other_3], f32)
    side_3 = list(zip([pack_3, other_3], halves, strict=True))
    f1, *halves = add_round(far, 2 * block, f1, [], [pack_4, other_4], bf16)
    side_4 = list(zip([pack_4, other_4], halves, strict=True))
    in_1 = swap(f1, move_r)
    (f2,) = add_round(far, 0, f2, side_3 + side_4, [], bf16)
    in_2 = swap(f2, move_r)

    sides = side_2 + side_3 + side_4
    (n,) = add_round(near, 2 * block, n, sides, [], f32)
    from_q = swap((n[:block] + in_1[:block].astype(f32)).astype(bf16), move_q)
    from_qp = swap((n[block:] + in_1[block:].astype(f32)).astype(bf16), move_q, move_p)
    (beside,) = add_round(near, block, beside, sides, [], f32)
    from_p = swap((beside + in_2[block:].astype(f32)).astype(bf16), move_p)
    (total,) = add_round(near, 0, total, sides, [], f32)
    total = total + diag + in_2[:block].astype(f32)
    return total + from_q.astype(f32) + from_qp.astype(f32) + from_p.astype(f32)


def solution(mesh):
    return jax.shard_map(
        on_device,
        mesh=mesh,
        in_specs=(P(("row", "col"), None), P(), P(("row", "col")), P(("row", "col"), None)),
        out_specs=P(("row", "col"), None),
        check_vma=False,
    )
```

```python
import math

import jax
import jax.numpy as jnp
from jax import lax
from jax.experimental import pallas as pl
from jax.experimental.pallas import tpu as pltpu
from jax.sharding import PartitionSpec as P


ROOT_LOG2E = math.sqrt(math.log2(math.e))
NT = (((1,), (1,)), ((), ()))
LANES = 128
HALF = 64
BLOCK = 384
AXES = ("row", "col")
VMEM = pl.BlockSpec(memory_space=pltpu.VMEM)


def place(x, y, z, core):
    return ((y % 2) * 8 + x * 2 + core) * 8 + (y // 2) * 4 + z


def swap(value, *steps):
    pairs = []
    for x in range(4):
        for y in range(4):
            for z in range(4):
                for core in range(2):
                    to = {"x": x, "y": y, "z": z}
                    for step in steps:
                        axis, flip = step[core]
                        to[axis] ^= flip
                    pairs.append((place(x, y, z, core), place(to["x"], to["y"], to["z"], core)))
    return lax.ppermute(value, AXES, pairs)


def partner(value):
    return lax.ppermute(value, AXES, [(i, i ^ 8) for i in range(128)])


def augment(pair, is_col):
    count = pair.shape[0]
    wide = pair.astype(jnp.float32)
    swapped = pltpu.roll(wide, HALF, 1)
    whole = wide + swapped
    norm = jnp.sum(whole * whole, axis=1, keepdims=True) * -0.25
    first = norm.astype(jnp.bfloat16).astype(jnp.float32)
    rest = norm - first
    second = rest.astype(jnp.bfloat16).astype(jnp.float32)
    third = rest - second
    lane = lax.broadcasted_iota(jnp.int32, (count, LANES), 1)
    at, ones = (HALF + 3, HALF) if is_col else (HALF, HALF + 3)
    extra = jnp.where((lane >= ones) & (lane < ones + 3), 1.0, 0.0)
    extra = jnp.where(lane == at, first, extra)
    extra = jnp.where(lane == at + 1, second, extra)
    extra = jnp.where(lane == at + 2, third, extra)
    low = lane < HALF
    if is_col:
        return pair, jnp.where(low, wide, extra).astype(jnp.bfloat16)
    return jnp.where(low, wide, swapped).astype(jnp.bfloat16), jnp.where(low, swapped, extra).astype(jnp.bfloat16)


def pack_own(embeddings_t, inv_length, probes):
    block, width = probes.shape

    def body(emb_hbm, inv_hbm, probe_hbm, own_ref, pair_ref, emb_ref, inv_ref, sems):
        copies = [
            pltpu.make_async_copy(emb_hbm, emb_ref, sems.at[0]),
            pltpu.make_async_copy(inv_hbm, inv_ref, sems.at[1]),
            pltpu.make_async_copy(probe_hbm, own_ref.at[:, LANES:], sems.at[2]),
        ]
        for copy in copies:
            copy.start()
        copies[0].wait()
        copies[1].wait()
        emb = emb_ref[...]
        twice = jnp.concatenate([emb, emb], axis=0).T
        inv = inv_ref[...]
        scaled = (twice * jnp.concatenate([inv, inv], axis=1)) * ROOT_LOG2E
        high = scaled.astype(jnp.bfloat16).astype(jnp.float32)
        lane = lax.broadcasted_iota(jnp.int32, (block, LANES), 1)
        pair = jnp.where(lane < HALF, high, scaled - high).astype(jnp.bfloat16)
        pair_ref[...] = pair
        own_ref[:, :LANES] = pair
        copies[2].wait()

    return pl.pallas_call(
        body,
        in_specs=[pl.BlockSpec(memory_space=pltpu.HBM)] * 3,
        out_specs=[VMEM] * 2,
        out_shape=[
            jax.ShapeDtypeStruct((block, LANES + width), jnp.bfloat16),
            jax.ShapeDtypeStruct((block, LANES), jnp.bfloat16),
        ],
        scratch_shapes=[
            pltpu.VMEM(embeddings_t.shape, jnp.float32),
            pltpu.VMEM(inv_length.shape, jnp.float32),
            pltpu.SemaphoreType.DMA((3,)),
        ],
        compiler_params=pltpu.CompilerParams(vmem_limit_bytes=64900 << 10),
        name="pack_own",
    )(embeddings_t, inv_length, probes)


def join(first, *others):
    count, width = others[0].shape

    def body(*refs):
        out_ref = refs[-1]
        out_ref[:count, :] = refs[0][:, :width]
        for i, ref in enumerate(refs[1:-1], 1):
            out_ref[i * count : (i + 1) * count, :] = ref[...]

    return pl.pallas_call(
        body,
        in_specs=[VMEM] * (1 + len(others)),
        out_specs=VMEM,
        out_shape=jax.ShapeDtypeStruct(((1 + len(others)) * count, width), first.dtype),
        compiler_params=pltpu.CompilerParams(vmem_limit_bytes=8 << 20),
    )(first, *others)


def params(mib):
    return pltpu.CompilerParams(vmem_limit_bytes=mib << 20)


def cost(rows, cols, width):
    return pl.CostEstimate(
        flops=4 * rows * cols * 2 * LANES, transcendentals=rows * cols, bytes_accessed=4 * rows * width
    )


def fold(row_ref, at, column, probe):
    gram = lax.dot_general(row_ref[at, :], column, NT, preferred_element_type=jnp.float32)
    return jnp.dot(jnp.exp2(gram).astype(jnp.bfloat16), probe, preferred_element_type=jnp.float32)


def fill_rows(pair_ref, left):
    for k in range(0, pair_ref.shape[0], BLOCK):
        a, b = augment(pair_ref[k : k + BLOCK, :], False)
        left[k : k + BLOCK, :LANES] = a
        left[k : k + BLOCK, LANES:] = b


def fill_columns(pack_refs, right, probes):
    start = 0
    for src in pack_refs:
        for k in range(0, src.shape[0], BLOCK):
            a, b = augment(src[k : k + BLOCK, :LANES], True)
            right[start : start + BLOCK, :LANES] = a
            right[start : start + BLOCK, LANES:] = b
            probes[start : start + BLOCK, :] = src[k : k + BLOCK, LANES:]
            start += BLOCK


def columns_shape(packs):
    cols = sum(q.shape[0] for q in packs)
    width = packs[0].shape[1] - LANES
    return [jax.ShapeDtypeStruct((cols, 2 * LANES), jnp.bfloat16), jax.ShapeDtypeStruct((cols, width), jnp.bfloat16)]


def take_pair(own):
    def body(own_ref, out_ref):
        out_ref[...] = own_ref[:, :LANES]

    return pl.pallas_call(
        body,
        in_specs=[VMEM],
        out_specs=VMEM,
        out_shape=half_of(own),
        compiler_params=params(8),
        name="take_pair",
    )(own)


def half_of(pack):
    return jax.ShapeDtypeStruct((pack.shape[0], LANES), jnp.bfloat16)


def prepare_rows(pairs):
    def body(pair_ref, left):
        fill_rows(pair_ref, left)

    return pl.pallas_call(
        body,
        in_specs=[VMEM],
        out_specs=VMEM,
        out_shape=jax.ShapeDtypeStruct((pairs.shape[0], 2 * LANES), jnp.bfloat16),
        compiler_params=params(12),
    )(pairs)


def near_round(rows, packs):
    count = rows.shape[0]
    shape = columns_shape(packs)
    width = shape[1].shape[1]
    sizes = (BLOCK, BLOCK, 2 * BLOCK)

    def body(*refs):
        row_ref, pack_refs, (own_ref, beside_ref, rest_ref, right, probes) = refs[0], refs[1:-5], refs[-5:]
        fill_columns(pack_refs, right, probes)
        part = fold(row_ref, pl.ds(0, 2 * BLOCK), right[...], probes[...])
        own_ref[...] = part[:BLOCK, :]
        beside_ref[...] = part[BLOCK:, :]
        rest_ref[...] = fold(row_ref, pl.ds(2 * BLOCK, 2 * BLOCK), right[...], probes[...])

    return pl.pallas_call(
        body,
        in_specs=[VMEM] * (1 + len(packs)),
        out_specs=[VMEM] * 5,
        out_shape=[jax.ShapeDtypeStruct((size, width), jnp.float32) for size in sizes] + shape,
        cost_estimate=cost(count, shape[0].shape[0], width),
        compiler_params=params(28),
    )(rows, *packs)


def far_round(pairs, columns):
    count, width, step = pairs.shape[0], columns[0][1].shape[1], 2 * BLOCK
    flat = [x for side in columns for x in side]

    def body(*refs):
        pair_ref, rest, (left, *outs) = refs[0], refs[1:-3], refs[-3:]
        fill_rows(pair_ref, left)
        for i, ref in enumerate(outs):
            at = pl.ds(i * step, step)
            part = fold(left, at, rest[0][...], rest[1][...])
            for k in range(2, len(rest), 2):
                part = part + fold(left, at, rest[k][...], rest[k + 1][...])
            ref[...] = part

    return pl.pallas_call(
        body,
        in_specs=[VMEM] * (1 + len(flat)),
        out_specs=[VMEM] * 3,
        out_shape=[jax.ShapeDtypeStruct((count, 2 * LANES), jnp.bfloat16)]
        + [jax.ShapeDtypeStruct((step, width), jnp.float32)] * 2,
        cost_estimate=cost(count, sum(side[0].shape[0] for side in columns), width),
        compiler_params=params(28),
    )(pairs, *flat)


def far_more(rows, olds, packs):
    shape, step, n = columns_shape(packs), olds[0].shape[0], len(olds)

    def body(*refs):
        row_ref, old_refs, pack_refs = refs[0], refs[1 : 1 + n], refs[1 + n : 1 + n + len(packs)]
        outs, (right, probes) = refs[-2 - n : -2], refs[-2:]
        fill_columns(pack_refs, right, probes)
        for i in range(n):
            outs[i][...] = old_refs[i][...] + fold(row_ref, pl.ds(i * step, step), right[...], probes[...])

    return pl.pallas_call(
        body,
        in_specs=[VMEM] * (1 + n + len(packs)),
        out_specs=[VMEM] * (n + 2),
        out_shape=[jax.ShapeDtypeStruct(old.shape, jnp.float32) for old in olds] + shape,
        cost_estimate=cost(n * step, shape[0].shape[0], olds[0].shape[1]),
        compiler_params=params(28),
    )(rows, *olds, *packs)


def accumulate(rows, at, old, packs, out_type):
    count, width = old.shape
    shape = columns_shape(packs)

    def body(*refs):
        row_ref, old_ref, pack_refs, (out_ref, right, probes) = refs[0], refs[1], refs[2:-3], refs[-3:]
        fill_columns(pack_refs, right, probes)
        part = fold(row_ref, pl.ds(at, count), right[...], probes[...])
        out_ref[...] = (old_ref[...] + part).astype(out_type)

    return pl.pallas_call(
        body,
        in_specs=[VMEM] * (2 + len(packs)),
        out_specs=[VMEM] * 3,
        out_shape=[jax.ShapeDtypeStruct((count, width), out_type)] + shape,
        cost_estimate=cost(count, shape[0].shape[0], width),
        compiler_params=params(28),
    )(rows, old, *packs)


def apply_rows(rows, at, old, columns, out_type):
    count, width = old.shape
    flat = [a for pair in columns for a in pair]

    def body(*refs):
        row_ref, old_ref, rest, out_ref = refs[0], refs[1], refs[2:-1], refs[-1]
        part = old_ref[...]
        for k in range(0, len(rest), 2):
            part = part + fold(row_ref, pl.ds(at, count), rest[k][...], rest[k + 1][...])
        out_ref[...] = part.astype(out_type)

    return pl.pallas_call(
        body,
        in_specs=[VMEM] * (2 + len(flat)),
        out_specs=VMEM,
        out_shape=jax.ShapeDtypeStruct((count, width), out_type),
        cost_estimate=cost(count, sum(c[0].shape[0] for c in columns), width),
        compiler_params=params(28),
    )(rows, old, *flat)


COL_MOVES = ((("x", 1), ("x", 3)), (("x", 3), ("y", 1)), (("y", 1), ("x", 1)))
ROW_MOVES = ((("z", 1), ("z", 3)), (("z", 3), ("y", 3)), (("y", 3), ("z", 1)))


def diagonal(noise, probes):
    return lax.optimization_barrier(noise[:, None] * probes.astype(jnp.float32))


def on_device(embeddings, inv_length, noise, probes):
    block = probes.shape[0]
    f32, bf16 = jnp.float32, jnp.bfloat16
    move_a, move_b, move_c = COL_MOVES
    move_p, move_q, move_r = ROW_MOVES
    own, pair = pack_own(embeddings.T, inv_length[None, :], probes)
    diag = diagonal(noise, probes)

    got_a = swap(own, move_a)
    got_ab = swap(own, move_b, move_a)
    got_b = swap(own, move_b)
    rows_p = swap(pair, move_p)
    rows_q = swap(pair, move_q)
    rows_qp = swap(pair, move_q, move_p)
    four = join(own, got_a, got_b, got_ab)
    pack_c = swap(four, move_c)
    near_pair = take_pair(own)
    quads = join(near_pair, rows_p, rows_q, rows_qp)
    rows_r = swap(quads, move_r)
    pack_a, pack_b = join(own, got_a), join(got_b, got_ab)
    other_a, other_b = partner(pack_a), partner(pack_b)

    near = prepare_rows(quads)
    total, beside, n, *aug_a = near_round(near, [pack_a, other_a])
    n, *aug_b = accumulate(near, 2 * block, n, [pack_b, other_b], f32)
    far, f2, f1 = far_round(rows_r, [aug_a, aug_b])
    other_c = partner(pack_c)
    f2, f1, *aug_c = far_more(far, [f2, f1], [pack_c])
    f1, *aug_d = accumulate(far, 2 * block, f1, [other_c], bf16)
    in_1 = swap(f1, move_r)
    f2 = apply_rows(far, 0, f2, [aug_d], bf16)
    in_2 = swap(f2, move_r)

    columns = [aug_b, aug_c, aug_d]
    n = apply_rows(near, 2 * block, n, columns[1:], f32)
    from_q = swap((n[:block] + in_1[:block].astype(f32)).astype(bf16), move_q)
    from_qp = swap((n[block:] + in_1[block:].astype(f32)).astype(bf16), move_q, move_p)
    beside = apply_rows(near, block, beside, columns, f32)
    from_p = swap((beside + in_2[block:].astype(f32)).astype(bf16), move_p)
    total = apply_rows(near, 0, total, columns, f32)
    total = total + diag + in_2[:block].astype(f32)
    return total + from_q.astype(f32) + from_qp.astype(f32) + from_p.astype(f32)


def solution(mesh):
    return jax.shard_map(
        on_device,
        mesh=mesh,
        in_specs=(P(("row", "col"), None), P(), P(("row", "col")), P(("row", "col"), None)),
        out_specs=P(("row", "col"), None),
        check_vma=False,
    )
```

```python
import math

import jax
import jax.numpy as jnp
from jax import lax
from jax.experimental import pallas as pl
from jax.experimental.pallas import tpu as pltpu
from jax.sharding import PartitionSpec as P


ROOT_LOG2E = math.sqrt(math.log2(math.e))
NT = (((1,), (1,)), ((), ()))
LANES = 128
HALF = 64
BLOCK = 384
AXES = ("row", "col")
VMEM = pl.BlockSpec(memory_space=pltpu.VMEM)


def place(x, y, z, core):
    return ((y % 2) * 8 + x * 2 + core) * 8 + (y // 2) * 4 + z


def swap(value, *steps):
    pairs = []
    for x in range(4):
        for y in range(4):
            for z in range(4):
                for core in range(2):
                    to = {"x": x, "y": y, "z": z}
                    for step in steps:
                        axis, flip = step[core]
                        to[axis] ^= flip
                    pairs.append((place(x, y, z, core), place(to["x"], to["y"], to["z"], core)))
    return lax.ppermute(value, AXES, pairs)


def partner(value):
    return lax.ppermute(value, AXES, [(i, i ^ 8) for i in range(128)])


def augment(pair, is_col):
    count = pair.shape[0]
    wide = pair.astype(jnp.float32)
    swapped = pltpu.roll(wide, HALF, 1)
    whole = wide + swapped
    norm = jnp.sum(whole * whole, axis=1, keepdims=True) * -0.25
    first = norm.astype(jnp.bfloat16).astype(jnp.float32)
    rest = norm - first
    second = rest.astype(jnp.bfloat16).astype(jnp.float32)
    third = rest - second
    lane = lax.broadcasted_iota(jnp.int32, (count, LANES), 1)
    at, ones = (HALF + 3, HALF) if is_col else (HALF, HALF + 3)
    extra = jnp.where((lane >= ones) & (lane < ones + 3), 1.0, 0.0)
    extra = jnp.where(lane == at, first, extra)
    extra = jnp.where(lane == at + 1, second, extra)
    extra = jnp.where(lane == at + 2, third, extra)
    low = lane < HALF
    if is_col:
        return pair, jnp.where(low, wide, extra).astype(jnp.bfloat16)
    return jnp.where(low, wide, swapped).astype(jnp.bfloat16), jnp.where(low, swapped, extra).astype(jnp.bfloat16)


def pack_own(embeddings_t, inv_length, probes):
    block, width = probes.shape

    def body(emb_hbm, inv_hbm, probe_hbm, own_ref, pair_ref, emb_ref, inv_ref, sems):
        copies = [
            pltpu.make_async_copy(emb_hbm, emb_ref, sems.at[0]),
            pltpu.make_async_copy(inv_hbm, inv_ref, sems.at[1]),
            pltpu.make_async_copy(probe_hbm, own_ref.at[:, LANES:], sems.at[2]),
        ]
        for copy in copies:
            copy.start()
        copies[0].wait()
        copies[1].wait()
        emb = emb_ref[...]
        twice = jnp.concatenate([emb, emb], axis=0).T
        inv = inv_ref[...]
        scaled = (twice * jnp.concatenate([inv, inv], axis=1)) * ROOT_LOG2E
        high = scaled.astype(jnp.bfloat16).astype(jnp.float32)
        lane = lax.broadcasted_iota(jnp.int32, (block, LANES), 1)
        pair = jnp.where(lane < HALF, high, scaled - high).astype(jnp.bfloat16)
        pair_ref[...] = pair
        own_ref[:, :LANES] = pair
        copies[2].wait()

    return pl.pallas_call(
        body,
        in_specs=[pl.BlockSpec(memory_space=pltpu.HBM)] * 3,
        out_specs=[VMEM] * 2,
        out_shape=[
            jax.ShapeDtypeStruct((block, LANES + width), jnp.bfloat16),
            jax.ShapeDtypeStruct((block, LANES), jnp.bfloat16),
        ],
        scratch_shapes=[
            pltpu.VMEM(embeddings_t.shape, jnp.float32),
            pltpu.VMEM(inv_length.shape, jnp.float32),
            pltpu.SemaphoreType.DMA((3,)),
        ],
        compiler_params=pltpu.CompilerParams(vmem_limit_bytes=64900 << 10),
        name="pack_own",
    )(embeddings_t, inv_length, probes)


def join(first, *others):
    count, width = others[0].shape

    def body(*refs):
        out_ref = refs[-1]
        out_ref[:count, :] = refs[0][:, :width]
        for i, ref in enumerate(refs[1:-1], 1):
            out_ref[i * count : (i + 1) * count, :] = ref[...]

    return pl.pallas_call(
        body,
        in_specs=[VMEM] * (1 + len(others)),
        out_specs=VMEM,
        out_shape=jax.ShapeDtypeStruct(((1 + len(others)) * count, width), first.dtype),
        compiler_params=pltpu.CompilerParams(vmem_limit_bytes=8 << 20),
    )(first, *others)


def params(mib):
    return pltpu.CompilerParams(vmem_limit_bytes=mib << 20)


def cost(rows, cols, width):
    return pl.CostEstimate(
        flops=4 * rows * cols * 2 * LANES, transcendentals=rows * cols, bytes_accessed=4 * rows * width
    )


def fold(row_ref, at, column, probe):
    gram = lax.dot_general(row_ref[at, :], column, NT, preferred_element_type=jnp.float32)
    return jnp.dot(jnp.exp2(gram).astype(jnp.bfloat16), probe, preferred_element_type=jnp.float32)


def fill_rows(pair_ref, left):
    for k in range(0, pair_ref.shape[0], BLOCK):
        a, b = augment(pair_ref[k : k + BLOCK, :], False)
        left[k : k + BLOCK, :LANES] = a
        left[k : k + BLOCK, LANES:] = b


def fill_columns(pack_refs, right, probes):
    start = 0
    for src in pack_refs:
        for k in range(0, src.shape[0], BLOCK):
            a, b = augment(src[k : k + BLOCK, :LANES], True)
            right[start : start + BLOCK, :LANES] = a
            right[start : start + BLOCK, LANES:] = b
            probes[start : start + BLOCK, :] = src[k : k + BLOCK, LANES:]
            start += BLOCK


def columns_shape(packs):
    cols = sum(q.shape[0] for q in packs)
    width = packs[0].shape[1] - LANES
    return [jax.ShapeDtypeStruct((cols, 2 * LANES), jnp.bfloat16), jax.ShapeDtypeStruct((cols, width), jnp.bfloat16)]


def prepare_rows(pairs):
    def body(pair_ref, left):
        fill_rows(pair_ref, left)

    return pl.pallas_call(
        body,
        in_specs=[VMEM],
        out_specs=VMEM,
        out_shape=jax.ShapeDtypeStruct((pairs.shape[0], 2 * LANES), jnp.bfloat16),
        compiler_params=params(12),
    )(pairs)


def near_round(rows, packs):
    count = rows.shape[0]
    shape = columns_shape(packs)
    width = shape[1].shape[1]
    sizes = (BLOCK, BLOCK, 2 * BLOCK)

    def body(*refs):
        row_ref, pack_refs, (own_ref, beside_ref, rest_ref, right, probes) = refs[0], refs[1:-5], refs[-5:]
        fill_columns(pack_refs, right, probes)
        part = fold(row_ref, pl.ds(0, 2 * BLOCK), right[...], probes[...])
        own_ref[...] = part[:BLOCK, :]
        beside_ref[...] = part[BLOCK:, :]
        rest_ref[...] = fold(row_ref, pl.ds(2 * BLOCK, 2 * BLOCK), right[...], probes[...])

    return pl.pallas_call(
        body,
        in_specs=[VMEM] * (1 + len(packs)),
        out_specs=[VMEM] * 5,
        out_shape=[jax.ShapeDtypeStruct((size, width), jnp.float32) for size in sizes] + shape,
        cost_estimate=cost(count, shape[0].shape[0], width),
        compiler_params=params(28),
    )(rows, *packs)


def far_round(pairs, columns):
    count, width, step = pairs.shape[0], columns[1].shape[1], 2 * BLOCK

    def body(pair_ref, right, probes, left, first_ref, second_ref):
        fill_rows(pair_ref, left)
        for i, ref in enumerate((first_ref, second_ref)):
            ref[...] = fold(left, pl.ds(i * step, step), right[...], probes[...])

    return pl.pallas_call(
        body,
        in_specs=[VMEM] * 3,
        out_specs=[VMEM] * 3,
        out_shape=[jax.ShapeDtypeStruct((count, 2 * LANES), jnp.bfloat16)]
        + [jax.ShapeDtypeStruct((step, width), jnp.float32)] * 2,
        cost_estimate=cost(count, columns[0].shape[0], width),
        compiler_params=params(28),
    )(pairs, *columns)


def accumulate(rows, at, old, packs, out_type):
    count, width = old.shape
    shape = columns_shape(packs)

    def body(*refs):
        row_ref, old_ref, pack_refs, (out_ref, right, probes) = refs[0], refs[1], refs[2:-3], refs[-3:]
        fill_columns(pack_refs, right, probes)
        part = fold(row_ref, pl.ds(at, count), right[...], probes[...])
        out_ref[...] = (old_ref[...] + part).astype(out_type)

    return pl.pallas_call(
        body,
        in_specs=[VMEM] * (2 + len(packs)),
        out_specs=[VMEM] * 3,
        out_shape=[jax.ShapeDtypeStruct((count, width), out_type)] + shape,
        cost_estimate=cost(count, shape[0].shape[0], width),
        compiler_params=params(28),
    )(rows, old, *packs)


def apply_rows(rows, at, old, columns, out_type):
    count, width = old.shape
    flat = [a for pair in columns for a in pair]

    def body(*refs):
        row_ref, old_ref, rest, out_ref = refs[0], refs[1], refs[2:-1], refs[-1]
        part = old_ref[...]
        for k in range(0, len(rest), 2):
            part = part + fold(row_ref, pl.ds(at, count), rest[k][...], rest[k + 1][...])
        out_ref[...] = part.astype(out_type)

    return pl.pallas_call(
        body,
        in_specs=[VMEM] * (2 + len(flat)),
        out_specs=VMEM,
        out_shape=jax.ShapeDtypeStruct((count, width), out_type),
        cost_estimate=cost(count, sum(c[0].shape[0] for c in columns), width),
        compiler_params=params(28),
    )(rows, old, *flat)


COL_MOVES = ((("x", 1), ("x", 3)), (("x", 3), ("y", 1)), (("y", 1), ("x", 1)))
ROW_MOVES = ((("z", 1), ("z", 3)), (("z", 3), ("y", 3)), (("y", 3), ("z", 1)))


def diagonal(noise, probes):
    return lax.optimization_barrier(noise[:, None] * probes.astype(jnp.float32))


def on_device(embeddings, inv_length, noise, probes):
    block = probes.shape[0]
    f32, bf16 = jnp.float32, jnp.bfloat16
    move_a, move_b, move_c = COL_MOVES
    move_p, move_q, move_r = ROW_MOVES
    own, pair = pack_own(embeddings.T, inv_length[None, :], probes)
    diag = diagonal(noise, probes)

    got_a = swap(own, move_a)
    rows_p = swap(pair, move_p)
    rows_q = swap(pair, move_q)
    rows_qp = swap(pair, move_q, move_p)
    pack_a = join(own, got_a)
    pack_b = swap(pack_a, move_b)
    quads = join(own, rows_p, rows_q, rows_qp)
    rows_r = swap(quads, move_r)
    other_a = partner(pack_a)
    pack_c = swap(pack_a, move_c)

    near = prepare_rows(quads)
    total, beside, n, *aug_a = near_round(near, [pack_a, other_a])

    other_b, other_c = partner(pack_b), partner(pack_c)
    pack_d = swap(pack_b, move_c)
    far, f2, f1 = far_round(rows_r, aug_a)
    f1, *aug_b = accumulate(far, 2 * block, f1, [pack_b, other_b], f32)
    f1, *aug_c = accumulate(far, 2 * block, f1, [pack_c, other_c], f32)
    beside = apply_rows(near, block, beside, [aug_b], f32)
    other_d = partner(pack_d)
    f2 = apply_rows(far, 0, f2, [aug_b, aug_c], f32)
    f1, *aug_d = accumulate(far, 2 * block, f1, [pack_d, other_d], bf16)
    in_1 = swap(f1, move_r)
    f2 = apply_rows(far, 0, f2, [aug_d], bf16)
    in_2 = swap(f2, move_r)

    columns = [aug_b, aug_c, aug_d]
    n = apply_rows(near, 2 * block, n, columns, f32)
    from_q = swap((n[:block] + in_1[:block].astype(f32)).astype(bf16), move_q)
    from_qp = swap((n[block:] + in_1[block:].astype(f32)).astype(bf16), move_q, move_p)
    beside = apply_rows(near, block, beside, columns[1:], f32)
    from_p = swap((beside + in_2[block:].astype(f32)).astype(bf16), move_p)
    total = apply_rows(near, 0, total, columns, f32)
    total = total + diag + in_2[:block].astype(f32)
    return total + from_q.astype(f32) + from_qp.astype(f32) + from_p.astype(f32)


def solution(mesh):
    return jax.shard_map(
        on_device,
        mesh=mesh,
        in_specs=(P(("row", "col"), None), P(), P(("row", "col")), P(("row", "col"), None)),
        out_specs=P(("row", "col"), None),
        check_vma=False,
    )
```
